512 devices in a mesh: tp: 8 (over z), ep: 64 (over y, x, core).
Axes of the slice: x: 4, y: 8, z: 8, core: 2. Of those that a mesh axis runs over, the one named last changes fastest.
Arguments:
- attn: bfloat16 [32768, 1536], P('ep', 'tp'), may hold values from -6 to 6
- resid: bfloat16 [32768, 1536], P('ep', 'tp'), may hold values from -6 to 6
- w_out: bfloat16 [1536, 1536], P('tp', 'ep'), may hold values from -0.15625 to 0.15625
- gain_mix: float32 [1536], replicated, may hold values from 0.1 to 1.9
- gain_out: float32 [1536], replicated, may hold values from 0.1 to 1.9
- routes: int32 [32768, 8], P('ep'), may hold values from 0 to 39, all different within a row; in each aligned block of 64 rows (0 to 63, 64 to 127, ...) at most 16 rows name the same one
- gates: float32 [32768, 8], P('ep'), may hold values from 0.05 to 1
- w_gate: bfloat16 [64, 1536, 512], P('ep'), as said below
- w_up: bfloat16 [64, 1536, 512], P('ep'), as said below
- w_down: bfloat16 [64, 512, 1536], P('ep'), as said below
Outputs:
- layer_out: bfloat16 [32768, 1536], P('ep', 'tp')
The draws below stay inside these ranges and needn't reach their ends.
Inputs may be any that keep to these rules, and one draw needn't show every extreme that they name: `routes`: in each aligned block of 64 rows no expert is named more than 16 times; each row names 8 different experts. `w_gate`: copy s holds the weights of expert s % 40. `w_up`: copy s holds the weights of expert s % 40. `w_down`: copy s holds the weights of expert s % 40.
All inputs are finite; a program needn't handle non-finite values.
Results may differ from the reference program's by a relative error of at most 0.0053.
Values may be sent and summed in bfloat16 or wider, within the bound.
No kernel may reach another device: no remote copies, remote signals or barrier semaphores. Data moves between devices by JAX's collectives and lax.ppermute only.
A program may use at most 64 MiB of HBM per device.

```python
import math
import jax
import jax.numpy as jnp
import numpy as np
from jax import lax

D = 1536
FF = 512
EXPERTS = 40
TOPK = 8
TOKENS = 32768
BLOCK = 64
MOST = 16
SLOTS = 64


def expert_copies(key, shape, fan_in):
    expert_ids = jnp.arange(SLOTS) % EXPERTS

    def one_copy(expert):
        return jax.random.normal(jax.random.fold_in(key, expert), shape, jnp.float32) * fan_in ** (-0.5)
    return jax.vmap(one_copy)(expert_ids).astype(jnp.bfloat16)


def draw_w_gate(key, part):
    return expert_copies(jax.random.fold_in(key, 11), (D, FF), D)


def draw_w_up(key, part):
    return expert_copies(jax.random.fold_in(key, 23), (D, FF), D)


def draw_w_down(key, part):
    return expert_copies(jax.random.fold_in(key, 37), (FF, D), FF)


def shard_levels(key, shape, split, smallest, largest):
    loudness, own = 1.0, jax.random.fold_in(key, 6)
    for axis_at, parts in split:
        draws = jnp.exp(jax.random.uniform(jax.random.fold_in(own, axis_at), (parts,), jnp.float32, smallest / len(split), largest / len(split)))
        loudness = loudness * jnp.repeat(draws, shape[axis_at] // parts).reshape([-1 if axis == axis_at else 1 for axis in range(len(shape))])
    return loudness


def shared_out(own_key, own, number, rows, count, top, limit, lean):
    order = jax.random.permutation(own_key, count)
    crowded, usual = portions_of(count, rows * top, limit, lean, True), portions_of(count, rows * top, limit, lean, False)
    places = jnp.arange(count)

    def named(sizes, turn):
        used = int((sizes > 0).sum())
        fixed = max(1, used // 4)
        shifted = fixed + (places - fixed + turn * (used - fixed)) % max(1, count - fixed)
        return jnp.zeros((count,), jnp.int32).at[order[jnp.where(places < fixed, places, shifted)]].set(jnp.asarray(sizes, jnp.int32))

    sizes = jnp.where(number % 4 == 0, named(crowded, number // 4), named(usual, number - number // 4 - 1))
    mixed = jax.random.permutation(jax.random.fold_in(own, 3), count)
    giver, sink = mixed[0:count // 2 * 2:2], mixed[1:count // 2 * 2:2]
    margin = jnp.minimum(sizes[giver] - 1, limit - sizes[sink]) // 2
    margin = jnp.where((giver == order[0]) | (sink == order[0]) | (sizes[sink] == 0), 0, jnp.maximum(margin, 0))
    shifted = jax.random.randint(jax.random.fold_in(own, 4), (count // 2,), 0, 1 << 20) % (margin + 1)
    sizes = sizes.at[giver].add(-shifted).at[sink].add(shifted)
    items = jnp.searchsorted(jnp.cumsum(sizes), jnp.arange(rows * top), side="right").astype(jnp.int32)
    grid = items.reshape(top, rows).T
    grid = grid[jax.random.permutation(jax.random.fold_in(own, 1), rows)]
    turn = jax.random.randint(jax.random.fold_in(own, 2), (rows, 1), 0, top)
    return jnp.take_along_axis(grid, (jnp.arange(top)[None, :] + turn) % top, axis=1)


def portions_of(amount, total, reach, slope, full):
    loads = [(1 << 20) // math.isqrt(rank ** slope) + 1 for rank in range(1, amount + 1)]
    largest = reach if full else min(reach, max(-(-total // amount), total * loads[0] // sum(loads)))
    least = 1 if total - largest >= amount - 1 else 0
    holding, rest = [largest] + [least] * (amount - 1), total - largest - least * (amount - 1)
    while rest > 0:
        free = [i for i in range(1, amount) if holding[i] < largest] or [i for i in range(1, amount) if holding[i] < reach]
        whole, budget = sum([loads[i] for i in free]), rest
        for i in free:
            extra = min(reach - holding[i], max(1, budget * loads[i] // whole), rest)
            holding[i] = holding[i] + extra
            rest = rest - extra
    return np.array(holding)


def centred(stream_key, dims, spread, most, shards=(), held_as=jnp.bfloat16):
    factor_of = shard_levels(stream_key, dims, shards, -0.22, 0.18) if shards else 1.0
    result = jax.random.normal(stream_key, dims, jnp.float32) * spread * factor_of
    return jnp.minimum(jnp.maximum(result, -most), most).astype(held_as)


def setup_inputs(seed: int = 0) -> dict:
    key_list = jax.random.split(jax.random.key(seed), 11)
    attn = centred(key_list[0], (TOKENS, D), 1.0, 6.0, ((0, 64), (1, 8)))
    resid = centred(key_list[1], (TOKENS, D), 1.0, 6.0, ((0, 64), (1, 8)))
    w_out = centred(key_list[2], (D, D), D ** -0.5, 0.15625, ((0, 8), (1, 64)))
    gain_mix = jnp.clip(1.0 + 0.18 * jax.random.normal(key_list[3], (D,), jnp.float32), 0.1, 1.9)
    gain_out = jnp.clip(1.0 + 0.18 * jax.random.normal(key_list[4], (D,), jnp.float32), 0.1, 1.9)
    routes_keys = jax.random.split(jax.random.fold_in(key_list[5], 1), TOKENS // BLOCK)
    routes_turns = jax.random.permutation(jax.random.fold_in(key_list[5], 3), TOKENS // BLOCK)
    routes = jax.vmap(lambda own, number: shared_out(jax.random.fold_in(key_list[5], 2), own, number, BLOCK, EXPERTS, TOPK, MOST, 2))(routes_keys, routes_turns).reshape((TOKENS, TOPK))
    gates = jnp.clip(jnp.exp(math.log(1.0) - 2.9957323 * jax.random.uniform(key_list[6], (TOKENS, TOPK), jnp.float32) ** shard_levels(key_list[6], (TOKENS, TOPK), ((0, 64),), -0.2, 0.2)), 0.05, 1.0)
    w_gate = draw_w_gate(jax.random.fold_in(key_list[10], 71), 0)
    w_up = draw_w_up(jax.random.fold_in(key_list[10], 71), 0)
    w_down = draw_w_down(jax.random.fold_in(key_list[10], 71), 0)
    return dict(attn=attn, resid=resid, w_out=w_out, gain_mix=gain_mix, gain_out=gain_out, routes=routes, gates=gates, w_gate=w_gate, w_up=w_up, w_down=w_down)


epsilon = 1e-05

def rms_scale(values, gain):
    return values * lax.rsqrt(lax.optimization_barrier(jnp.mean(values * values, axis=1, keepdims=True)) + epsilon) * gain

def reference(attn, resid, w_out, gain_mix, gain_out, routes, gates, w_gate, w_up, w_down):
    hidden = resid.astype(jnp.float32) + jnp.dot(attn, w_out, preferred_element_type=jnp.float32)
    normed = rms_scale(hidden, gain_mix).astype(jnp.bfloat16)
    capacity = TOKENS // BLOCK * MOST

    def one_expert(total, expert):
        hit = routes == expert
        weight = lax.optimization_barrier(jnp.sum(jnp.where(hit, gates, jnp.zeros_like(gates)), axis=1))
        routed = jnp.any(hit, axis=1)
        row_index = jnp.nonzero(routed, size=capacity, fill_value=0)[0].astype(jnp.int32)
        is_live = jnp.arange(capacity) < jnp.sum(routed.astype(jnp.int32))
        gathered = normed[row_index]
        gate_pre = jnp.dot(gathered, w_gate[expert], preferred_element_type=jnp.float32)
        up_pre = jnp.dot(gathered, w_up[expert], preferred_element_type=jnp.float32)
        activated = (jax.nn.silu(gate_pre) * up_pre).astype(jnp.bfloat16)
        expert_out = jnp.dot(activated, w_down[expert], preferred_element_type=jnp.float32).astype(jnp.bfloat16)
        scale_rows = jnp.where(is_live, weight[row_index], jnp.zeros_like(weight[row_index]))
        contrib = expert_out.astype(jnp.float32) * scale_rows[:, None]
        return (total.at[row_index].add(contrib), None)
    total, _ = lax.scan(one_expert, jnp.zeros(hidden.shape, jnp.float32), jnp.arange(EXPERTS, dtype=jnp.int32))
    combined = hidden + total
    return rms_scale(combined, gain_out).astype(jnp.bfloat16)
```

```python
import jax
import jax.numpy as jnp
from jax import lax
from jax.experimental import pallas as pl
from jax.experimental.pallas import tpu as pltpu
from jax.sharding import Mesh, PartitionSpec as P

EXPERTS = 40
CAP = 16
EPS = 1e-05
BF = jnp.bfloat16
F32 = jnp.float32
EP = ("h", "y", "x", "c")
VMEM = 56 * 1024 * 1024


def params():
    return pltpu.CompilerParams(vmem_limit_bytes=VMEM)


def dot(a, b, ca, cb):
    return lax.dot_general(a, b, (((ca,), (cb,)), ((), ())), preferred_element_type=F32)


def project_kernel(place_ref, attn_ref, resid_ref, w_ref, out_ref):
    tp = place_ref[4]
    weights = w_ref[...].reshape(1536, 192)
    at = lax.broadcasted_iota(jnp.int32, (1536, 192), 0)
    of = lax.broadcasted_iota(jnp.int32, (1536, 192), 1)
    choose = jnp.where(at == of + tp * 192, 1.0, 0.0).astype(BF)
    part = dot(attn_ref[...].T, weights, 1, 1) + dot(resid_ref[...].T, choose, 1, 1)
    out_ref[...] = part.astype(BF).reshape(8, 64, 1536)


def piece_kernel(place_ref, wg_ref, wu_ref, wd_ref, out_ref):
    out_ref[0:192, :] = wg_ref[0]
    out_ref[192:384, :] = wu_ref[0]
    for i in range(3):
        out_ref[384 + i * 64 : 448 + i * 64, :] = wd_ref[0, :, i * 512 : (i + 1) * 512]


def one_hot_rows(routed, expert, rank_of):
    hits = jnp.zeros((routed.shape[0], expert.shape[1]), F32)
    for k in range(8):
        hits = hits + jnp.where(routed[:, k : k + 1] == expert, 1.0, 0.0)
    ranks = dot(rank_of, hits.astype(BF), 1, 0)
    return hits, ranks


def before_matrix(rows):
    a = lax.broadcasted_iota(jnp.int32, (rows, rows), 0)
    b = lax.broadcasted_iota(jnp.int32, (rows, rows), 1)
    keep = (b < a) & (a // 64 == b // 64)
    return jnp.where(keep, 1.0, 0.0).astype(BF)


def lane_experts(place_ref, lane):
    half, me = place_ref[3], place_ref[5]
    slot = lane // CAP
    near = (32 * half + slot) % EXPERTS
    far = 32 - 8 * half + (me + slot) % 8
    return jnp.where(slot < 32, near, far).astype(F32)


def mix_kernel(place_ref, part_ref, routes_ref, gain_ref, send_ref, hid_ref, *far_refs):
    hidden = part_ref[0].astype(F32)
    for z in range(1, 8):
        hidden = hidden + part_ref[z].astype(F32)
    hid_ref[...] = hidden
    mean = jnp.sum(hidden * hidden, axis=1, keepdims=True) / 1536
    normed = (hidden * lax.rsqrt(mean + EPS) * gain_ref[...]).astype(BF)
    lane = lax.broadcasted_iota(jnp.int32, (1, 640), 1)
    hits, ranks = one_hot_rows(routes_ref[...].astype(F32), lane_experts(place_ref, lane), before_matrix(64))
    pick = jnp.where(ranks == (lane % CAP).astype(F32), hits, 0.0).astype(BF)
    far = dot(pick[:, 512:640], normed, 0, 0).astype(BF)
    for k in range(8):
        far_refs[k][...] = far[k * CAP : (k + 1) * CAP]
    send_ref[...] = dot(pick[:, 0:512], normed, 0, 0).astype(BF).reshape(32, CAP, 1536)


def expert(x, w_gate, w_up, w_down):
    gate = dot(x, w_gate, 1, 0)
    up = dot(x, w_up, 1, 0)
    act = (gate / (1.0 + jnp.exp(-gate)) * up).astype(BF)
    return dot(act, w_down, 1, 0).astype(BF)


def near_kernel(x_ref, wg_ref, wu_ref, wd_ref, out_ref):
    y = expert(x_ref[...].reshape(256, 1536), wg_ref[0], wu_ref[0], wd_ref[0])
    out_ref[...] = y.reshape(16, CAP, 1536)


def far_kernel(*refs):
    x_refs, w_ref, out_refs, (wg_scr, wu_scr, wd_scr) = refs[0:8], refs[8], refs[9:17], refs[17:]
    for z in range(8):
        wg_scr[z * 192 : (z + 1) * 192, :] = w_ref[z, 0:192, :]
        wu_scr[z * 192 : (z + 1) * 192, :] = w_ref[z, 192:384, :]
        for i in range(3):
            wd_scr[z * 64 : (z + 1) * 64, i * 512 : (i + 1) * 512] = w_ref[z, 384 + i * 64 : 448 + i * 64, :]
    x = jnp.concatenate([ref[...] for ref in x_refs], axis=0)
    y = expert(x, wg_scr[...], wu_scr[...], wd_scr[...])
    for k in range(8):
        out_refs[k][...] = y[k * CAP : (k + 1) * CAP]


def close_kernel(place_ref, routes_ref, gates_ref, hid_ref, gain_ref, near_ref, *refs):
    far_refs, out_ref = refs[0:8], refs[8]
    lane = lax.broadcasted_iota(jnp.int32, (1, 640), 1)
    expert_of = lane_experts(place_ref, lane)
    routed = routes_ref[...].astype(F32)
    hits, ranks = one_hot_rows(routed, expert_of, before_matrix(64))
    gate = jnp.zeros((64, 640), F32)
    for k in range(8):
        gate = gate + jnp.where(routed[:, k : k + 1] == expert_of, gates_ref[:, k : k + 1], 0.0)
    gate = jnp.where((ranks == (lane % CAP).astype(F32)) & (hits > 0.5), gate, 0.0)
    high = gate.astype(BF)
    low = (gate - high.astype(F32)).astype(BF)
    both = jnp.concatenate([high, low], axis=0)
    far = jnp.concatenate([ref[...] for ref in far_refs], axis=0)
    total = dot(both[:, 0:512], near_ref[...].reshape(512, 1536), 1, 0) + dot(both[:, 512:640], far, 1, 0)
    combined = hid_ref[...] + (total[0:64] + total[64:128])
    mean = jnp.sum(combined * combined, axis=1, keepdims=True) / 1536
    out = (combined * lax.rsqrt(mean + EPS) * gain_ref[...]).astype(BF)
    for z in range(8):
        out_ref[z] = out[:, z * 192 : (z + 1) * 192]


def smem():
    return pl.BlockSpec(memory_space=pltpu.SMEM)


def vmem():
    return pl.BlockSpec(memory_space=pltpu.VMEM)


def per_device(attn, resid, w_out, gain_mix, gain_out, routes, gates, w_gate, w_up, w_down):
    tp, h, y = lax.axis_index("tp"), lax.axis_index("h"), lax.axis_index("y")
    core, me = lax.axis_index("c"), lax.axis_index(("x", "c"))
    place = jnp.stack([core, h * 4 + y, y, h, tp, me])
    shape = jax.ShapeDtypeStruct
    my_routes = lax.dynamic_slice_in_dim(routes, tp * 64, 64, 0)
    my_gates = lax.dynamic_slice_in_dim(gates, tp * 64, 64, 0)

    piece = pl.pallas_call(
        piece_kernel,
        grid_spec=pltpu.PrefetchScalarGridSpec(
            num_scalar_prefetch=1,
            grid=(1,),
            in_specs=[
                pl.BlockSpec((1, 192, 512), lambda i, p: (0, p[4], 0)),
                pl.BlockSpec((1, 192, 512), lambda i, p: (0, p[4], 0)),
                pl.BlockSpec((1, 64, 1536), lambda i, p: (0, p[4], 0)),
            ],
            out_specs=pl.BlockSpec((576, 512), lambda i, p: (0, 0)),
        ),
        out_shape=shape((576, 512), BF),
        compiler_params=params(),
        name="piece",
    )(place, w_gate, w_up, w_down)
    crossed = lax.ppermute(piece, ("h", "y"), [(4, 3), (3, 4)])
    columns = lax.all_to_all(jnp.broadcast_to(w_out.T[None], (64, 24, 192)), EP, 0, 0, tiled=True)
    crossed, _ = lax.optimization_barrier((crossed, columns))
    pieces = lax.all_gather(crossed, "y", axis=0, tiled=False)

    parts = pl.pallas_call(
        project_kernel,
        out_shape=shape((8, 64, 1536), BF),
        in_specs=[smem()] + [vmem()] * 3,
        out_specs=vmem(),
        compiler_params=params(),
        name="project",
    )(place, attn.T, resid.T, columns)
    parts = lax.all_to_all(parts, "tp", 0, 0, tiled=True)
    rows = shape((CAP, 1536), BF)
    send, hidden, *far = pl.pallas_call(
        mix_kernel,
        out_shape=(shape((32, CAP, 1536), BF), shape((64, 1536), F32)) + (rows,) * 8,
        in_specs=[smem()] + [vmem()] * 3,
        out_specs=(vmem(),) * 10,
        compiler_params=params(),
        name="mix",
    )(place, parts, my_routes, gain_mix.reshape(1, 1536))

    pieces, _ = lax.optimization_barrier((pieces, send))
    far_piece = lax.dynamic_index_in_dim(pieces, 3 - 3 * h, 0, keepdims=False)
    far_weights = lax.all_gather(far_piece, "tp", axis=0, tiled=False)

    shift = lambda v, k: lax.ppermute(v, ("x", "c"), [(i, (i + k) % 8) for i in range(8)])
    far = far[0:1] + [shift(far[k], k) for k in range(1, 8)]
    received = lax.all_to_all(send, ("y", "x", "c"), 0, 0, tiled=True)
    received, far = lax.optimization_barrier((received, far))

    whole = lambda *dims: pl.BlockSpec(dims, lambda i: (0,) * len(dims))
    near = pl.pallas_call(
        near_kernel,
        grid=(2,),
        out_shape=shape((32, CAP, 1536), BF),
        in_specs=[
            pl.BlockSpec((16, CAP, 1536), lambda i: (i, 0, 0)),
            whole(1, 1536, 512),
            whole(1, 1536, 512),
            whole(1, 512, 1536),
        ],
        out_specs=pl.BlockSpec((16, CAP, 1536), lambda i: (i, 0, 0)),
        compiler_params=params(),
        name="near",
    )(received, w_gate, w_up, w_down)
    far = pl.pallas_call(
        far_kernel,
        out_shape=(rows,) * 8,
        in_specs=[vmem()] * 9,
        out_specs=(vmem(),) * 8,
        scratch_shapes=[pltpu.VMEM((1536, 512), BF), pltpu.VMEM((1536, 512), BF), pltpu.VMEM((512, 1536), BF)],
        compiler_params=params(),
        name="far",
    )(*far, far_weights)
    near = lax.all_to_all(near, ("y", "x", "c"), 0, 0, tiled=True)
    far = [far[0]] + [shift(far[k], 8 - k) for k in range(1, 8)]

    finished = pl.pallas_call(
        close_kernel,
        out_shape=shape((8, 64, 192), BF),
        in_specs=[smem()] + [vmem()] * 13,
        out_specs=vmem(),
        compiler_params=params(),
        name="close",
    )(place, my_routes, my_gates, hidden, gain_out.reshape(1, 1536), near, *far)
    return lax.all_to_all(finished, "tp", 0, 0, tiled=True).reshape(512, 192)


def solution(mesh):
    fine = Mesh(mesh.devices.reshape(8, 2, 4, 4, 2), ("tp",) + EP)
    return jax.shard_map(
        per_device,
        mesh=fine,
        in_specs=(
            P(EP, "tp"),
            P(EP, "tp"),
            P("tp", EP),
            P(),
            P(),
            P(EP, None),
            P(EP, None),
            P(EP, None, None),
            P(EP, None, None),
            P(EP, None, None),
        ),
        out_specs=P(EP, "tp"),
        check_vma=False,
    )
```

```python
import jax
import jax.numpy as jnp
from jax import lax
from jax.experimental import pallas as pl
from jax.experimental.pallas import tpu as pltpu
from jax.sharding import Mesh, PartitionSpec as P

EXPERTS = 40
CAP = 16
EPS = 1e-05
BF = jnp.bfloat16
F32 = jnp.float32
EP = ("h", "y", "x", "c")
VMEM = 56 * 1024 * 1024


def params():
    return pltpu.CompilerParams(vmem_limit_bytes=VMEM)


def dot(a, b, ca, cb):
    return lax.dot_general(a, b, (((ca,), (cb,)), ((), ())), preferred_element_type=F32)


def project_kernel(place_ref, attn_ref, resid_ref, w_ref, out_ref, w_scr):
    tp = place_ref[1]
    for i in range(8):
        for y in range(8):
            w_scr[(y * 8 + i) * 24 : (y * 8 + i + 1) * 24, :] = w_ref[i, y * 24 : (y + 1) * 24, :]
    at = lax.broadcasted_iota(jnp.int32, (1536, 192), 0)
    of = lax.broadcasted_iota(jnp.int32, (1536, 192), 1)
    choose = jnp.where(at == of + tp * 192, 1.0, 0.0).astype(BF)
    part = dot(attn_ref[...].T, w_scr[...], 1, 1) + dot(resid_ref[...].T, choose, 1, 1)
    out_ref[...] = part.astype(BF).reshape(8, 64, 1536)


def piece_kernel(place_ref, wg_ref, wu_ref, wd_ref, out_ref):
    out_ref[0:192, :] = wg_ref[0]
    out_ref[192:384, :] = wu_ref[0]
    for i in range(3):
        out_ref[384 + i * 64 : 448 + i * 64, :] = wd_ref[0, :, i * 512 : (i + 1) * 512]


def one_hot_rows(routed, expert, rank_of):
    hits = jnp.zeros((routed.shape[0], expert.shape[1]), F32)
    for k in range(8):
        hits = hits + jnp.where(routed[:, k : k + 1] == expert, 1.0, 0.0)
    ranks = dot(rank_of, hits.astype(BF), 1, 0)
    return hits, ranks


def before_matrix(rows):
    a = lax.broadcasted_iota(jnp.int32, (rows, rows), 0)
    b = lax.broadcasted_iota(jnp.int32, (rows, rows), 1)
    keep = (b < a) & (a // 64 == b // 64)
    return jnp.where(keep, 1.0, 0.0).astype(BF)


def lanes_of(half):
    lane = lax.broadcasted_iota(jnp.int32, (1, 768), 1)
    near = lane < 512
    far_lane = lane - 512
    expert_of = jnp.where(near, (32 * half + lane // CAP) % EXPERTS, 32 - 8 * half + (far_lane // 8) % 8)
    want = jnp.where(near, lane % CAP, 4 * (far_lane // 64) + lane % 4)
    copy = jnp.where(near, 2, (lane % 8) // 4)
    return expert_of.astype(F32), want.astype(F32), copy


def upper_copy(rows, columns):
    return lax.broadcasted_iota(jnp.int32, (rows, columns), 0) % 8 < 4


def near_to_wire(values, ref, slots):
    for k in range(12):
        ref[:, k * CAP : (k + 1) * CAP, :] = values[:, k * 128 : (k + 1) * 128].reshape(slots, CAP, 128)


def near_from_wire(ref, slots):
    parts = [ref[:, k * CAP : (k + 1) * CAP, :].reshape(slots * CAP, 128) for k in range(12)]
    return jnp.concatenate(parts, axis=1)


def far_to_wire(values, ref, start):
    upper = upper_copy(256, 128)
    for m in range(6):
        even, odd = values[:, m * 256 : m * 256 + 128], values[:, m * 256 + 128 : m * 256 + 256]
        ref[:, start + m * 8 : start + m * 8 + 8, :] = jnp.where(upper, even, odd).astype(BF).reshape(32, 8, 128)


def mix_kernel(place_ref, part_ref, routes_ref, gain_ref, send_ref, hid_ref):
    hidden = part_ref[0].astype(F32)
    for z in range(1, 8):
        hidden = hidden + part_ref[z].astype(F32)
    hid_ref[...] = hidden
    mean = jnp.sum(hidden * hidden, axis=1, keepdims=True) / 1536
    normed = (hidden * lax.rsqrt(mean + EPS) * gain_ref[...]).astype(BF)
    expert_of, want, _ = lanes_of(place_ref[0])
    hits, ranks = one_hot_rows(routes_ref[...].astype(F32), expert_of, before_matrix(64))
    pick = jnp.where(ranks == want, hits, 0.0).astype(BF)
    near_to_wire(dot(pick[:, 0:512], normed, 0, 0).astype(BF), send_ref, 32)
    far_to_wire(dot(pick[:, 512:768], normed, 0, 0), send_ref, 192)


def act(gate, up):
    return (gate / (1.0 + jnp.exp(-gate)) * up).astype(BF)


def near_kernel(x_ref, wg_ref, wu_ref, wd_ref, out_ref):
    x = near_from_wire(x_ref, 16)
    y = dot(act(dot(x, wg_ref[0], 1, 0), dot(x, wu_ref[0], 1, 0)), wd_ref[0], 1, 0)
    near_to_wire(y.astype(BF), out_ref, 16)


def far_kernel(place_ref, x_ref, *refs):
    w_refs, out_ref, (wg_scr, wu_scr, wd_scr) = refs[0:8], refs[9], refs[10:]
    tp = place_ref[1]
    for ref, away in zip(w_refs, (0, -1, 1, -2, 2, -3, 3, -4)):
        z = (tp + away + 8) % 8
        wide, thin = pl.ds(pl.multiple_of(z * 192, 64), 192), pl.ds(pl.multiple_of(z * 64, 64), 64)
        wg_scr[wide, :] = ref[0:192, :]
        wu_scr[wide, :] = ref[192:384, :]
        for i in range(3):
            wd_scr[thin, i * 512 : (i + 1) * 512] = ref[384 + i * 64 : 448 + i * 64, :]
    x = jnp.concatenate([x_ref[:, m * 8 : m * 8 + 8, :].reshape(256, 128) for m in range(6)], axis=1)
    upper = upper_copy(256, 512)

    def whole(scr):
        even = jnp.concatenate([scr[m * 256 : m * 256 + 128, :] for m in range(6)], axis=0)
        odd = jnp.concatenate([scr[m * 256 + 128 : m * 256 + 256, :] for m in range(6)], axis=0)
        a, b = dot(x, even, 1, 0), dot(x, odd, 1, 0)
        return jnp.where(upper, a + pltpu.roll(b, 252, 0), b + pltpu.roll(a, 4, 0))

    far_to_wire(dot(act(whole(wg_scr), whole(wu_scr)), wd_scr[...], 1, 0), out_ref, 0)


def close_kernel(place_ref, routes_ref, gates_ref, hid_ref, gain_ref, got_ref, out_ref):
    expert_of, want, copy = lanes_of(place_ref[0])
    routed = routes_ref[...].astype(F32)
    hits, ranks = one_hot_rows(routed, expert_of, before_matrix(64))
    gate = jnp.zeros((64, 768), F32)
    for k in range(8):
        gate = gate + jnp.where(routed[:, k : k + 1] == expert_of, gates_ref[:, k : k + 1], 0.0)
    gate = jnp.where((ranks == want) & (hits > 0.5), gate, 0.0)
    high = gate.astype(BF).astype(F32)
    both = jnp.concatenate([high, gate - high], axis=0)
    total = dot(both[:, 0:512].astype(BF), near_from_wire(got_ref, 32), 1, 0)
    far = both[:, 512:768]
    copies = [jnp.where(copy[:, 512:768] == u, far, 0.0) for u in range(2)]
    far = jnp.concatenate(copies, axis=0).astype(BF)
    chunks = []
    for m in range(6):
        part = dot(far, got_ref[:, 192 + m * 8 : 200 + m * 8, :].reshape(256, 128), 1, 0)
        chunks += [part[0:128], part[128:256]]
    total = total + jnp.concatenate(chunks, axis=1)
    combined = hid_ref[...] + (total[0:64] + total[64:128])
    mean = jnp.sum(combined * combined, axis=1, keepdims=True) / 1536
    out = (combined * lax.rsqrt(mean + EPS) * gain_ref[...]).astype(BF)
    for z in range(8):
        out_ref[z] = out[:, z * 192 : (z + 1) * 192]


def smem():
    return pl.BlockSpec(memory_space=pltpu.SMEM)


def vmem():
    return pl.BlockSpec(memory_space=pltpu.VMEM)


def per_device(attn, resid, w_out, gain_mix, gain_out, routes, gates, w_gate, w_up, w_down):
    tp, h = lax.axis_index("tp"), lax.axis_index("h")
    place = jnp.stack([h, tp])
    shape = jax.ShapeDtypeStruct
    my_routes = lax.dynamic_slice_in_dim(routes, tp * 64, 64, 0)
    my_gates = lax.dynamic_slice_in_dim(gates, tp * 64, 64, 0)

    piece = pl.pallas_call(
        piece_kernel,
        grid_spec=pltpu.PrefetchScalarGridSpec(
            num_scalar_prefetch=1,
            grid=(1,),
            in_specs=[
                pl.BlockSpec((1, 192, 512), lambda i, p: (0, p[1], 0)),
                pl.BlockSpec((1, 192, 512), lambda i, p: (0, p[1], 0)),
                pl.BlockSpec((1, 64, 1536), lambda i, p: (0, p[1], 0)),
            ],
            out_specs=pl.BlockSpec((576, 512), lambda i, p: (0, 0)),
        ),
        out_shape=shape((576, 512), BF),
        compiler_params=params(),
        name="piece",
    )(place, w_gate, w_up, w_down)
    across = lambda v, a, b, c, d: lax.ppermute(v, ("h", "y"), [(a, b), (c, d)])
    step_1 = across(piece, 4, 3, 3, 4)
    columns = lax.all_to_all(jnp.broadcast_to(w_out.T[None], (8, 24, 192)), ("h", "y"), 0, 0, tiled=True)
    columns = jnp.broadcast_to(columns.reshape(1, 192, 192), (8, 192, 192))
    columns = lax.all_to_all(columns, ("x", "c"), 0, 0, tiled=True)
    columns, step_1, piece = lax.optimization_barrier((columns, step_1, piece))
    step_2 = across(step_1, 3, 2, 4, 5)
    step_3 = across(piece, 4, 1, 3, 6)
    step_4 = across(step_3, 1, 0, 6, 7)

    parts = pl.pallas_call(
        project_kernel,
        out_shape=shape((8, 64, 1536), BF),
        in_specs=[smem()] + [vmem()] * 3,
        out_specs=vmem(),
        scratch_shapes=[pltpu.VMEM((1536, 192), BF)],
        compiler_params=params(),
        name="project",
    )(place, attn.T, resid.T, columns)
    parts = lax.all_to_all(parts, "tp", 0, 0, tiled=True)
    far_piece = (step_1 + step_2) + (step_3 + step_4)
    parts, far_piece = lax.optimization_barrier((parts, far_piece))

    turn = lambda v, d: lax.ppermute(v, "tp", [(i, (i + d) % 8) for i in range(8)])
    ring = [far_piece]
    up = down = far_piece
    for _ in range(3):
        up, down = turn(up, 1), turn(down, -1)
        ring += [up, down]
    ring.append(turn(up, 1))

    send, hidden = pl.pallas_call(
        mix_kernel,
        out_shape=(shape((32, 240, 128), BF), shape((64, 1536), F32)),
        in_specs=[smem()] + [vmem()] * 3,
        out_specs=(vmem(), vmem()),
        compiler_params=params(),
        name="mix",
    )(place, parts, my_routes, gain_mix.reshape(1, 1536))
    received = lax.all_to_all(send, ("y", "x", "c"), 0, 0, tiled=True)

    whole = lambda *dims: pl.BlockSpec(dims, lambda i: (0,) * len(dims))
    near = pl.pallas_call(
        near_kernel,
        grid=(2,),
        out_shape=shape((32, 240, 128), BF),
        in_specs=[
            pl.BlockSpec((16, 192, 128), lambda i: (i, 0, 0)),
            whole(1, 1536, 512),
            whole(1, 1536, 512),
            whole(1, 512, 1536),
        ],
        out_specs=pl.BlockSpec((16, 192, 128), lambda i: (i, 0, 0)),
        compiler_params=params(),
        name="near",
    )(received, w_gate, w_up, w_down)
    done = pl.pallas_call(
        far_kernel,
        grid=(1,),
        out_shape=shape((32, 240, 128), BF),
        in_specs=[smem(), pl.BlockSpec((32, 48, 128), lambda i: (0, 4, 0))]
        + [whole(576, 512)] * 8
        + [pl.BlockSpec(memory_space=pl.ANY)],
        out_specs=pl.BlockSpec((32, 48, 128), lambda i: (0, 4, 0)),
        scratch_shapes=[pltpu.VMEM((1536, 512), BF), pltpu.VMEM((1536, 512), BF), pltpu.VMEM((512, 1536), BF)],
        input_output_aliases={10: 0},
        compiler_params=params(),
        name="far",
    )(place, received, *ring, near)
    done = lax.all_to_all(done, ("y", "x", "c"), 0, 0, tiled=True)

    finished = pl.pallas_call(
        close_kernel,
        out_shape=shape((8, 64, 192), BF),
        in_specs=[smem()] + [vmem()] * 5,
        out_specs=vmem(),
        compiler_params=params(),
        name="close",
    )(place, my_routes, my_gates, hidden, gain_out.reshape(1, 1536), done)
    return lax.all_to_all(finished, "tp", 0, 0, tiled=True).reshape(512, 192)


def solution(mesh):
    fine = Mesh(mesh.devices.reshape(8, 2, 4, 4, 2), ("tp",) + EP)
    return jax.shard_map(
        per_device,
        mesh=fine,
        in_specs=(
            P(EP, "tp"),
            P(EP, "tp"),
            P("tp", EP),
            P(),
            P(),
            P(EP, None),
            P(EP, None),
            P(EP, None, None),
            P(EP, None, None),
            P(EP, None, None),
        ),
        out_specs=P(EP, "tp"),
        check_vma=False,
    )
```

```python
import jax
import jax.numpy as jnp
from jax import lax
from jax.experimental import pallas as pl
from jax.experimental.pallas import tpu as pltpu
from jax.sharding import Mesh, PartitionSpec as P

EXPERTS = 40
CAP = 16
EPS = 1e-05
BF = jnp.bfloat16
F32 = jnp.float32
EP = ("h", "y", "x", "c")
VMEM = 56 * 1024 * 1024


def params():
    return pltpu.CompilerParams(vmem_limit_bytes=VMEM)


def dot(a, b, ca, cb):
    return lax.dot_general(a, b, (((ca,), (cb,)), ((), ())), preferred_element_type=F32)


def project_kernel(place_ref, attn_ref, resid_ref, w_ref, out_ref):
    tp = place_ref[4]
    weights = w_ref[...].reshape(1536, 192)
    at = lax.broadcasted_iota(jnp.int32, (1536, 192), 0)
    of = lax.broadcasted_iota(jnp.int32, (1536, 192), 1)
    choose = jnp.where(at == of + tp * 192, 1.0, 0.0).astype(BF)
    part = dot(attn_ref[...].T, weights, 1, 1) + dot(resid_ref[...].T, choose, 1, 1)
    out_ref[...] = part.astype(BF).reshape(8, 64, 1536)


def piece_kernel(place_ref, wg_ref, wu_ref, wd_ref, out_ref):
    out_ref[0:192, :] = wg_ref[0]
    out_ref[192:384, :] = wu_ref[0]
    for i in range(3):
        out_ref[384 + i * 64 : 448 + i * 64, :] = wd_ref[0, :, i * 512 : (i + 1) * 512]


def one_hot_rows(routed, expert, rank_of):
    hits = jnp.zeros((routed.shape[0], expert.shape[1]), F32)
    for k in range(8):
        hits = hits + jnp.where(routed[:, k : k + 1] == expert, 1.0, 0.0)
    ranks = dot(rank_of, hits.astype(BF), 1, 0)
    return hits, ranks


def before_matrix(rows):
    a = lax.broadcasted_iota(jnp.int32, (rows, rows), 0)
    b = lax.broadcasted_iota(jnp.int32, (rows, rows), 1)
    keep = (b < a) & (a // 64 == b // 64)
    return jnp.where(keep, 1.0, 0.0).astype(BF)


def lane_experts(place_ref, lane):
    half, me = place_ref[3], place_ref[5]
    slot = lane // CAP
    near = (32 * half + slot) % EXPERTS
    far = 32 - 8 * half + (me + slot) % 8
    return jnp.where(slot < 32, near, far).astype(F32)


def mix_kernel(place_ref, part_ref, routes_ref, gain_ref, send_ref, hid_ref, *far_refs):
    hidden = part_ref[0].astype(F32)
    for z in range(1, 8):
        hidden = hidden + part_ref[z].astype(F32)
    hid_ref[...] = hidden
    mean = jnp.sum(hidden * hidden, axis=1, keepdims=True) / 1536
    normed = (hidden * lax.rsqrt(mean + EPS) * gain_ref[...]).astype(BF)
    lane = lax.broadcasted_iota(jnp.int32, (1, 640), 1)
    hits, ranks = one_hot_rows(routes_ref[...].astype(F32), lane_experts(place_ref, lane), before_matrix(64))
    pick = jnp.where(ranks == (lane % CAP).astype(F32), hits, 0.0).astype(BF)
    far = dot(pick[:, 512:640], normed, 0, 0).astype(BF)
    for k in range(8):
        far_refs[k][...] = far[k * CAP : (k + 1) * CAP]
    send_ref[...] = dot(pick[:, 0:512], normed, 0, 0).astype(BF).reshape(32, CAP, 1536)


def expert(x, w_gate, w_up, w_down):
    gate = dot(x, w_gate, 1, 0)
    up = dot(x, w_up, 1, 0)
    act = (gate / (1.0 + jnp.exp(-gate)) * up).astype(BF)
    return dot(act, w_down, 1, 0).astype(BF)


def near_kernel(x_ref, wg_ref, wu_ref, wd_ref, out_ref):
    y = expert(x_ref[...].reshape(256, 1536), wg_ref[0], wu_ref[0], wd_ref[0])
    out_ref[...] = y.reshape(16, CAP, 1536)


def far_kernel(place_ref, *refs):
    x_refs, w_refs, out_refs, (wg_scr, wu_scr, wd_scr) = refs[0:8], refs[8:16], refs[16:24], refs[24:]
    tp = place_ref[4]
    for ref, away in zip(w_refs, (0, -1, 1, -2, 2, -3, 3, -4)):
        z = (tp + away + 8) % 8
        wide, thin = pl.ds(pl.multiple_of(z * 192, 64), 192), pl.ds(pl.multiple_of(z * 64, 64), 64)
        wg_scr[wide, :] = ref[0:192, :]
        wu_scr[wide, :] = ref[192:384, :]
        for i in range(3):
            wd_scr[thin, i * 512 : (i + 1) * 512] = ref[384 + i * 64 : 448 + i * 64, :]
    x = jnp.concatenate([ref[...] for ref in x_refs], axis=0)
    y = expert(x, wg_scr[...], wu_scr[...], wd_scr[...])
    for k in range(8):
        out_refs[k][...] = y[k * CAP : (k + 1) * CAP]


def close_kernel(place_ref, routes_ref, gates_ref, hid_ref, gain_ref, near_ref, *refs):
    far_refs, out_ref = refs[0:8], refs[8]
    lane = lax.broadcasted_iota(jnp.int32, (1, 640), 1)
    expert_of = lane_experts(place_ref, lane)
    routed = routes_ref[...].astype(F32)
    hits, ranks = one_hot_rows(routed, expert_of, before_matrix(64))
    gate = jnp.zeros((64, 640), F32)
    for k in range(8):
        gate = gate + jnp.where(routed[:, k : k + 1] == expert_of, gates_ref[:, k : k + 1], 0.0)
    gate = jnp.where((ranks == (lane % CAP).astype(F32)) & (hits > 0.5), gate, 0.0)
    high = gate.astype(BF)
    low = (gate - high.astype(F32)).astype(BF)
    both = jnp.concatenate([high, low], axis=0)
    far = jnp.concatenate([ref[...] for ref in far_refs], axis=0)
    total = dot(both[:, 0:512], near_ref[...].reshape(512, 1536), 1, 0) + dot(both[:, 512:640], far, 1, 0)
    combined = hid_ref[...] + (total[0:64] + total[64:128])
    mean = jnp.sum(combined * combined, axis=1, keepdims=True) / 1536
    out = (combined * lax.rsqrt(mean + EPS) * gain_ref[...]).astype(BF)
    for z in range(8):
        out_ref[z] = out[:, z * 192 : (z + 1) * 192]


def smem():
    return pl.BlockSpec(memory_space=pltpu.SMEM)


def vmem():
    return pl.BlockSpec(memory_space=pltpu.VMEM)


def keep(value):
    return pltpu.with_memory_space_constraint(value, pltpu.VMEM)


def per_device(attn, resid, w_out, gain_mix, gain_out, routes, gates, w_gate, w_up, w_down):
    tp, h, y = lax.axis_index("tp"), lax.axis_index("h"), lax.axis_index("y")
    core, me = lax.axis_index("c"), lax.axis_index(("x", "c"))
    place = jnp.stack([core, h * 4 + y, y, h, tp, me])
    shape = jax.ShapeDtypeStruct
    my_routes = lax.dynamic_slice_in_dim(routes, tp * 64, 64, 0)
    my_gates = lax.dynamic_slice_in_dim(gates, tp * 64, 64, 0)

    piece = pl.pallas_call(
        piece_kernel,
        grid_spec=pltpu.PrefetchScalarGridSpec(
            num_scalar_prefetch=1,
            grid=(1,),
            in_specs=[
                pl.BlockSpec((1, 192, 512), lambda i, p: (0, p[4], 0)),
                pl.BlockSpec((1, 192, 512), lambda i, p: (0, p[4], 0)),
                pl.BlockSpec((1, 64, 1536), lambda i, p: (0, p[4], 0)),
            ],
            out_specs=pl.BlockSpec((576, 512), lambda i, p: (0, 0)),
        ),
        out_shape=shape((576, 512), BF),
        compiler_params=params(),
        name="piece",
    )(place, w_gate, w_up, w_down)
    across = lambda v, a, b, c, d: lax.ppermute(v, ("h", "y"), [(a, b), (c, d)])
    step_1 = across(piece, 4, 3, 3, 4)
    step_3 = across(piece, 4, 1, 3, 6)
    columns = lax.all_to_all(jnp.broadcast_to(w_out.T[None], (64, 24, 192)), EP, 0, 0, tiled=True)
    columns, step_1, step_3 = lax.optimization_barrier((columns, step_1, step_3))
    step_2 = across(step_1, 3, 2, 4, 5)
    step_4 = across(step_3, 1, 0, 6, 7)

    parts = pl.pallas_call(
        project_kernel,
        out_shape=shape((8, 64, 1536), BF),
        in_specs=[smem()] + [vmem()] * 3,
        out_specs=vmem(),
        compiler_params=params(),
        name="project",
    )(place, attn.T, resid.T, keep(columns))
    parts = lax.all_to_all(parts, "tp", 0, 0, tiled=True)
    far_piece = (step_1 + step_2) + (step_3 + step_4)
    turn = lambda v, d: lax.ppermute(v, "tp", [(i, (i + d) % 8) for i in range(8)])
    up, down = turn(far_piece, 1), turn(far_piece, -1)
    parts, up, down = lax.optimization_barrier((parts, up, down))
    ring = [far_piece, up, down]

    rows = shape((CAP, 1536), BF)
    send, hidden, *far = pl.pallas_call(
        mix_kernel,
        out_shape=(shape((32, CAP, 1536), BF), shape((64, 1536), F32)) + (rows,) * 8,
        in_specs=[smem()] + [vmem()] * 3,
        out_specs=(vmem(),) * 10,
        compiler_params=params(),
        name="mix",
    )(place, keep(parts), my_routes, gain_mix.reshape(1, 1536))

    shift = lambda v, k: lax.ppermute(v, ("x", "c"), [(i, (i + k) % 8) for i in range(8)])
    far = far[0:1] + [shift(far[k], k) for k in range(1, 8)]
    received = lax.all_to_all(send, ("y", "x", "c"), 0, 0, tiled=True)
    for _ in range(2):
        up, down = turn(up, 1), turn(down, -1)
        ring += [up, down]
    received, far, ring = lax.optimization_barrier((received, far, ring))
    ring.append(turn(ring[5], 1))

    whole = lambda *dims: pl.BlockSpec(dims, lambda i: (0,) * len(dims))
    near = pl.pallas_call(
        near_kernel,
        grid=(2,),
        out_shape=shape((32, CAP, 1536), BF),
        in_specs=[
            pl.BlockSpec((16, CAP, 1536), lambda i: (i, 0, 0)),
            whole(1, 1536, 512),
            whole(1, 1536, 512),
            whole(1, 512, 1536),
        ],
        out_specs=pl.BlockSpec((16, CAP, 1536), lambda i: (i, 0, 0)),
        compiler_params=params(),
        name="near",
    )(received, w_gate, w_up, w_down)
    far = pl.pallas_call(
        far_kernel,
        out_shape=(rows,) * 8,
        in_specs=[smem()] + [vmem()] * 16,
        out_specs=(vmem(),) * 8,
        scratch_shapes=[pltpu.VMEM((1536, 512), BF), pltpu.VMEM((1536, 512), BF), pltpu.VMEM((512, 1536), BF)],
        compiler_params=params(),
        name="far",
    )(place, *far, *ring)
    near = lax.all_to_all(near, ("y", "x", "c"), 0, 0, tiled=True)
    far = [far[0]] + [shift(far[k], 8 - k) for k in range(1, 8)]

    finished = pl.pallas_call(
        close_kernel,
        out_shape=shape((8, 64, 192), BF),
        in_specs=[smem()] + [vmem()] * 13,
        out_specs=vmem(),
        compiler_params=params(),
        name="close",
    )(place, my_routes, my_gates, hidden, gain_out.reshape(1, 1536), keep(near), *far)
    return lax.all_to_all(finished, "tp", 0, 0, tiled=True).reshape(512, 192)


def solution(mesh):
    fine = Mesh(mesh.devices.reshape(8, 2, 4, 4, 2), ("tp",) + EP)
    return jax.shard_map(
        per_device,
        mesh=fine,
        in_specs=(
            P(EP, "tp"),
            P(EP, "tp"),
            P("tp", EP),
            P(),
            P(),
            P(EP, None),
            P(EP, None),
            P(EP, None, None),
            P(EP, None, None),
            P(EP, None, None),
        ),
        out_specs=P(EP, "tp"),
        check_vma=False,
    )
```

```python
import jax
import jax.numpy as jnp
from jax import lax
from jax.experimental import pallas as pl
from jax.experimental.pallas import tpu as pltpu
from jax.sharding import Mesh, PartitionSpec as P

EXPERTS = 40
CAP = 16
EPS = 1e-05
BF = jnp.bfloat16
F32 = jnp.float32
EP = ("h", "y", "x", "c")
VMEM = 56 * 1024 * 1024


def params():
    return pltpu.CompilerParams(vmem_limit_bytes=VMEM)


def dot(a, b, ca, cb):
    return lax.dot_general(a, b, (((ca,), (cb,)), ((), ())), preferred_element_type=F32)


def pack_kernel(attn_ref, resid_ref, w_ref, out_ref):
    both = jnp.concatenate([attn_ref[...], resid_ref[...]], axis=0)
    turned = both.T
    out_ref[:, 0:64, :] = turned.reshape(8, 64, 384)
    for i in range(8):
        out_ref[i, 64:88, 192:384] = jnp.zeros((24, 192), BF)
        out_ref[i, 64:88, 0:192] = w_ref[...]


def unpack_kernel(got_ref, routes_ref, tok_ref, w_ref):
    for z in range(8):
        at = z * 192
        tok_ref[:, at : at + 192] = got_ref[z, 0:64, 0:192]
        tok_ref[:, 1536 + at : 1728 + at] = got_ref[z, 0:64, 192:384]
        for y in range(8):
            w_ref[y, :, at : at + 192] = got_ref[z, 64:88, 0:192]
    tok_ref[:, 3072:3200] = jnp.zeros((64, 128), BF)
    tok_ref[:, 3072:3080] = routes_ref[...].astype(F32).astype(BF)


def piece_kernel(place_ref, wg_ref, wu_ref, wd_ref, out_ref):
    out_ref[0:192, :] = wg_ref[0]
    out_ref[192:384, :] = wu_ref[0]
    for i in range(3):
        out_ref[384 + i * 64 : 448 + i * 64, :] = wd_ref[0, :, i * 512 : (i + 1) * 512]


def one_hot_rows(routed, expert, rank_of):
    hits = jnp.zeros((routed.shape[0], expert.shape[1]), F32)
    for k in range(8):
        hits = hits + jnp.where(routed[:, k : k + 1] == expert, 1.0, 0.0)
    ranks = dot(rank_of, hits.astype(BF), 1, 0)
    return hits, ranks


def before_matrix(rows):
    a = lax.broadcasted_iota(jnp.int32, (rows, rows), 0)
    b = lax.broadcasted_iota(jnp.int32, (rows, rows), 1)
    keep = (b < a) & (a // 64 == b // 64)
    return jnp.where(keep, 1.0, 0.0).astype(BF)


def mix_kernel(place_ref, tok_ref, wa_ref, wb_ref, gain_ref, send_ref, hid_ref, w_scr, h_scr, n_scr):
    core, row, local = place_ref[0], place_ref[1], place_ref[2]
    for ref, off in ((wa_ref, core * 24), (wb_ref, (1 - core) * 24)):
        for y in range(8):
            for x in range(4):
                at = pl.multiple_of((y * 4 + x) * 48 + off, 8)
                w_scr[pl.ds(at, 24), :] = ref[x, y * 24 : (y + 1) * 24, :]
    total = jnp.zeros((256, 1), F32)
    attn = tok_ref[:, 0:1536]
    for n in range(0, 1536, 256):
        part = dot(attn, w_scr[n : n + 256, :], 1, 1) + tok_ref[:, 1536 + n : 1792 + n].astype(F32)
        h_scr[:, n : n + 256] = part
        total = total + jnp.sum(part * part, axis=1, keepdims=True)
    scale = lax.rsqrt(total / 1536 + EPS)
    n_scr[...] = (h_scr[...] * scale * gain_ref[...]).astype(BF)

    lane = lax.broadcasted_iota(jnp.int32, (1, 128), 1)
    slot = lane // CAP
    want = (lane % CAP).astype(F32)
    near = ((8 * row + slot) % EXPERTS).astype(F32)
    far = (jnp.where(row < 4, 32, 24) + slot).astype(F32)
    routed = tok_ref[:, 3072:3200].astype(F32)
    hits, ranks = one_hot_rows(routed, near, before_matrix(256))
    pick = jnp.where(ranks == want, hits, 0.0).astype(BF)
    for b in range(4):
        rows = dot(pick[b * 64 : (b + 1) * 64], n_scr[b * 64 : (b + 1) * 64, :], 0, 0)
        send_ref[:, b * CAP : (b + 1) * CAP, :] = rows.astype(BF).reshape(8, CAP, 1536)
    mine = pl.ds(pl.multiple_of(local * 64, 64), 64)
    hits, ranks = one_hot_rows(tok_ref[mine, 3072:3200].astype(F32), far, before_matrix(64))
    pick = jnp.where(ranks == want, hits, 0.0).astype(BF)
    rows = dot(pick, n_scr[mine, :], 0, 0)
    send_ref[:, 64:80, :] = rows.astype(BF).reshape(8, CAP, 1536)
    hid_ref[...] = h_scr[mine, :]


def expert(x, w_gate, w_up, w_down):
    gate = dot(x, w_gate, 1, 0)
    up = dot(x, w_up, 1, 0)
    act = (gate / (1.0 + jnp.exp(-gate)) * up).astype(BF)
    return dot(act, w_down, 1, 0).astype(BF)


def near_kernel(x_ref, wg_ref, wu_ref, wd_ref, out_ref):
    x = jnp.concatenate([x_ref[:, i * CAP : (i + 1) * CAP, :].reshape(128, 1536) for i in range(2)], axis=0)
    y = expert(x, wg_ref[0], wu_ref[0], wd_ref[0])
    out_ref[...] = y.reshape(2, 8, CAP, 1536)


def far_kernel(place_ref, x_ref, w_ref, *refs):
    out_refs, (wg_scr, wu_scr, wd_scr, y_scr) = refs[0:8], refs[8:]
    me = place_ref[5]
    for z in range(8):
        wg_scr[z * 192 : (z + 1) * 192, :] = w_ref[z, 0:192, :]
        wu_scr[z * 192 : (z + 1) * 192, :] = w_ref[z, 192:384, :]
        for i in range(3):
            wd_scr[z * 64 : (z + 1) * 64, i * 512 : (i + 1) * 512] = w_ref[z, 384 + i * 64 : 448 + i * 64, :]
    y_scr[...] = expert(x_ref[...].reshape(128, 1536), wg_scr[...], wu_scr[...], wd_scr[...])
    for k in range(8):
        out_refs[k][...] = y_scr[pl.ds(pl.multiple_of((me + k) % 8 * CAP, CAP), CAP), :]


def close_kernel(place_ref, routes_ref, gates_ref, hid_ref, gain_ref, near_ref, *refs):
    far_refs, out_ref = refs[0:8], refs[8]
    lane = lax.broadcasted_iota(jnp.int32, (1, 640), 1)
    half, me, slot = place_ref[3], place_ref[5], lane // CAP
    near_of, far_of = (32 * half + slot) % EXPERTS, 32 - 8 * half + (me + 40 - slot) % 8
    expert_of = jnp.where(slot < 32, near_of, far_of).astype(F32)
    routed = routes_ref[...].astype(F32)
    hits, ranks = one_hot_rows(routed, expert_of, before_matrix(64))
    gate = jnp.zeros((64, 640), F32)
    for k in range(8):
        gate = gate + jnp.where(routed[:, k : k + 1] == expert_of, gates_ref[:, k : k + 1], 0.0)
    gate = jnp.where((ranks == (lane % CAP).astype(F32)) & (hits > 0.5), gate, 0.0)
    high = gate.astype(BF)
    low = (gate - high.astype(F32)).astype(BF)
    both = jnp.concatenate([high, low], axis=0)
    far = jnp.concatenate([ref[...] for ref in far_refs], axis=0)
    total = dot(both[:, 0:512], near_ref[...].reshape(512, 1536), 1, 0) + dot(both[:, 512:640], far, 1, 0)
    combined = hid_ref[...] + (total[0:64] + total[64:128])
    mean = jnp.sum(combined * combined, axis=1, keepdims=True) / 1536
    out = (combined * lax.rsqrt(mean + EPS) * gain_ref[...]).astype(BF)
    for z in range(8):
        out_ref[z] = out[:, z * 192 : (z + 1) * 192]


def smem():
    return pl.BlockSpec(memory_space=pltpu.SMEM)


def vmem():
    return pl.BlockSpec(memory_space=pltpu.VMEM)


def keep(value):
    return pltpu.with_memory_space_constraint(value, pltpu.VMEM)


def per_device(attn, resid, w_out, gain_mix, gain_out, routes, gates, w_gate, w_up, w_down):
    tp, h, y = lax.axis_index("tp"), lax.axis_index("h"), lax.axis_index("y")
    core, me = lax.axis_index("c"), lax.axis_index(("x", "c"))
    place = jnp.stack([core, h * 4 + y, y, h, tp, me])
    shape = jax.ShapeDtypeStruct
    my_routes = lax.dynamic_slice_in_dim(routes, tp * 64, 64, 0)
    my_gates = lax.dynamic_slice_in_dim(gates, tp * 64, 64, 0)

    send = pl.pallas_call(
        pack_kernel,
        out_shape=shape((8, 88, 384), BF),
        in_specs=[vmem()] * 3,
        out_specs=vmem(),
        compiler_params=params(),
        name="pack",
    )(attn.T, resid.T, w_out.T)
    got = lax.all_to_all(send, "tp", 0, 0, tiled=True)

    piece = pl.pallas_call(
        piece_kernel,
        grid_spec=pltpu.PrefetchScalarGridSpec(
            num_scalar_prefetch=1,
            grid=(1,),
            in_specs=[
                pl.BlockSpec((1, 192, 512), lambda i, p: (0, p[4], 0)),
                pl.BlockSpec((1, 192, 512), lambda i, p: (0, p[4], 0)),
                pl.BlockSpec((1, 64, 1536), lambda i, p: (0, p[4], 0)),
            ],
            out_specs=pl.BlockSpec((576, 512), lambda i, p: (0, 0)),
        ),
        out_shape=shape((576, 512), BF),
        compiler_params=params(),
        name="piece",
    )(place, w_gate, w_up, w_down)
    across = lambda v, a, b, c, d: lax.ppermute(v, ("h", "y"), [(a, b), (c, d)])
    step_1 = across(piece, 4, 3, 3, 4)
    step_3 = across(piece, 4, 1, 3, 6)
    got, step_1 = lax.optimization_barrier((got, step_1))

    tokens, w_y = pl.pallas_call(
        unpack_kernel,
        out_shape=(shape((64, 3200), BF), shape((8, 24, 1536), BF)),
        in_specs=[vmem()] * 2,
        out_specs=(vmem(), vmem()),
        compiler_params=params(),
        name="unpack",
    )(keep(got), my_routes)
    tokens, w_y, step_3 = lax.optimization_barrier((tokens, w_y, step_3))
    tokens = lax.all_gather(tokens, "y", axis=0, tiled=True)
    w_y = lax.all_to_all(w_y, ("h", "y"), 0, 0, tiled=True)
    w_x = lax.all_to_all(jnp.broadcast_to(w_y.reshape(1, 192, 1536), (4, 192, 1536)), "x", 0, 0, tiled=True)
    w_x, tokens, step_1, step_3 = lax.optimization_barrier((w_x, tokens, step_1, step_3))
    w_c = lax.ppermute(w_x, "c", [(0, 1), (1, 0)])
    step_2 = across(step_1, 3, 2, 4, 5)
    step_4 = across(step_3, 1, 0, 6, 7)

    send, hidden = pl.pallas_call(
        mix_kernel,
        out_shape=(shape((8, 80, 1536), BF), shape((64, 1536), F32)),
        in_specs=[smem()] + [vmem()] * 4,
        out_specs=(vmem(), vmem()),
        scratch_shapes=[pltpu.VMEM((1536, 1536), BF), pltpu.VMEM((256, 1536), F32), pltpu.VMEM((256, 1536), BF)],
        compiler_params=params(),
        name="mix",
    )(place, tokens, w_x, w_c, gain_mix.reshape(1, 1536))
    step_2, step_4, _ = lax.optimization_barrier((step_2, step_4, send))
    far_piece = (step_1 + step_2) + (step_3 + step_4)
    far_weights = lax.all_gather(far_piece, "tp", axis=0, tiled=False)
    received = lax.all_to_all(send, ("x", "c"), 0, 0, tiled=True)

    whole = lambda *dims: pl.BlockSpec(dims, lambda i: (0,) * len(dims))
    near = pl.pallas_call(
        near_kernel,
        grid=(2,),
        out_shape=shape((4, 8, CAP, 1536), BF),
        in_specs=[
            pl.BlockSpec((8, 2 * CAP, 1536), lambda i: (0, i, 0)),
            whole(1, 1536, 512),
            whole(1, 1536, 512),
            whole(1, 512, 1536),
        ],
        out_specs=pl.BlockSpec((2, 8, CAP, 1536), lambda i: (i, 0, 0, 0)),
        compiler_params=params(),
        name="near",
    )(received, w_gate, w_up, w_down)
    near = lax.all_to_all(near.reshape(32, CAP, 1536), ("y", "x", "c"), 0, 0, tiled=True)
    far = pl.pallas_call(
        far_kernel,
        grid=(1,),
        out_shape=(shape((CAP, 1536), BF),) * 8,
        in_specs=[smem(), pl.BlockSpec((8, CAP, 1536), lambda i: (0, 4, 0))] + [whole(8, 576, 512)],
        out_specs=(whole(CAP, 1536),) * 8,
        scratch_shapes=[
            pltpu.VMEM((1536, 512), BF),
            pltpu.VMEM((1536, 512), BF),
            pltpu.VMEM((512, 1536), BF),
            pltpu.VMEM((128, 1536), BF),
        ],
        compiler_params=params(),
        name="far",
    )(place, received, far_weights)
    far = [far[0]] + [lax.ppermute(far[k], ("x", "c"), [(i, (i + k) % 8) for i in range(8)]) for k in range(1, 8)]

    finished = pl.pallas_call(
        close_kernel,
        out_shape=shape((8, 64, 192), BF),
        in_specs=[smem()] + [vmem()] * 13,
        out_specs=vmem(),
        compiler_params=params(),
        name="close",
    )(place, my_routes, my_gates, hidden, gain_out.reshape(1, 1536), keep(near), *far)
    return lax.all_to_all(finished, "tp", 0, 0, tiled=True).reshape(512, 192)


def solution(mesh):
    fine = Mesh(mesh.devices.reshape(8, 2, 4, 4, 2), ("tp",) + EP)
    return jax.shard_map(
        per_device,
        mesh=fine,
        in_specs=(
            P(EP, "tp"),
            P(EP, "tp"),
            P("tp", EP),
            P(),
            P(),
            P(EP, None),
            P(EP, None),
            P(EP, None, None),
            P(EP, None, None),
            P(EP, None, None),
        ),
        out_specs=P(EP, "tp"),
        check_vma=False,
    )
```

```python
import jax
import jax.numpy as jnp
from jax import lax
from jax.experimental import pallas as pl
from jax.experimental.pallas import tpu as pltpu
from jax.sharding import Mesh, PartitionSpec as P

EXPERTS = 40
CAP = 16
EPS = 1e-05
BF = jnp.bfloat16
F32 = jnp.float32
EP = ("h", "y", "x", "c")
VMEM = 56 * 1024 * 1024


def params():
    return pltpu.CompilerParams(vmem_limit_bytes=VMEM)


def dot(a, b, ca, cb):
    return lax.dot_general(a, b, (((ca,), (cb,)), ((), ())), preferred_element_type=F32)


def pack_kernel(attn_ref, resid_ref, w_ref, out_ref):
    both = jnp.concatenate([attn_ref[...], resid_ref[...]], axis=0)
    turned = both.T
    out_ref[:, 0:64, :] = turned.reshape(8, 64, 384)
    for i in range(8):
        out_ref[i, 64:88, 192:384] = jnp.zeros((24, 192), BF)
        out_ref[i, 64:88, 0:192] = w_ref[...]


def unpack_kernel(got_ref, routes_ref, tok_ref, w_ref):
    for z in range(8):
        at = z * 192
        tok_ref[:, at : at + 192] = got_ref[z, 0:64, 0:192]
        tok_ref[:, 1536 + at : 1728 + at] = got_ref[z, 0:64, 192:384]
        for y in range(8):
            w_ref[y, :, at : at + 192] = got_ref[z, 64:88, 0:192]
    tok_ref[:, 3072:3200] = jnp.zeros((64, 128), BF)
    tok_ref[:, 3072:3080] = routes_ref[...].astype(F32).astype(BF)


def piece_kernel(place_ref, wg_ref, wu_ref, wd_ref, out_ref):
    out_ref[0:192, :] = wg_ref[0]
    out_ref[192:384, :] = wu_ref[0]
    for i in range(3):
        out_ref[384 + i * 64 : 448 + i * 64, :] = wd_ref[0, :, i * 512 : (i + 1) * 512]


def one_hot_rows(routed, expert, rank_of):
    hits = jnp.zeros((routed.shape[0], expert.shape[1]), F32)
    for k in range(8):
        hits = hits + jnp.where(routed[:, k : k + 1] == expert, 1.0, 0.0)
    ranks = dot(rank_of, hits.astype(BF), 1, 0)
    return hits, ranks


def before_matrix(rows):
    a = lax.broadcasted_iota(jnp.int32, (rows, rows), 0)
    b = lax.broadcasted_iota(jnp.int32, (rows, rows), 1)
    keep = (b < a) & (a // 64 == b // 64)
    return jnp.where(keep, 1.0, 0.0).astype(BF)


def mix_kernel(place_ref, tok_ref, wa_ref, wb_ref, gain_ref, send_ref, hid_ref, w_scr, h_scr, n_scr):
    core, row, local = place_ref[0], place_ref[1], place_ref[2]
    for ref, off in ((wa_ref, core * 24), (wb_ref, (1 - core) * 24)):
        for y in range(8):
            for x in range(4):
                at = pl.multiple_of((y * 4 + x) * 48 + off, 8)
                w_scr[pl.ds(at, 24), :] = ref[x, y * 24 : (y + 1) * 24, :]
    total = jnp.zeros((256, 1), F32)
    attn = tok_ref[:, 0:1536]
    for n in range(0, 1536, 256):
        part = dot(attn, w_scr[n : n + 256, :], 1, 1) + tok_ref[:, 1536 + n : 1792 + n].astype(F32)
        h_scr[:, n : n + 256] = part
        total = total + jnp.sum(part * part, axis=1, keepdims=True)
    scale = lax.rsqrt(total / 1536 + EPS)
    n_scr[...] = (h_scr[...] * scale * gain_ref[...]).astype(BF)

    lane = lax.broadcasted_iota(jnp.int32, (1, 128), 1)
    slot = lane // CAP
    want = (lane % CAP).astype(F32)
    near = ((8 * row + slot) % EXPERTS).astype(F32)
    far = (jnp.where(row < 4, 32, 24) + slot).astype(F32)
    routed = tok_ref[:, 3072:3200].astype(F32)
    hits, ranks = one_hot_rows(routed, near, before_matrix(256))
    pick = jnp.where(ranks == want, hits, 0.0).astype(BF)
    for b in range(4):
        rows = dot(pick[b * 64 : (b + 1) * 64], n_scr[b * 64 : (b + 1) * 64, :], 0, 0)
        send_ref[:, b * CAP : (b + 1) * CAP, :] = rows.astype(BF).reshape(8, CAP, 1536)
    mine = pl.ds(pl.multiple_of(local * 64, 64), 64)
    hits, ranks = one_hot_rows(tok_ref[mine, 3072:3200].astype(F32), far, before_matrix(64))
    pick = jnp.where(ranks == want, hits, 0.0).astype(BF)
    rows = dot(pick, n_scr[mine, :], 0, 0)
    send_ref[:, 64:80, :] = rows.astype(BF).reshape(8, CAP, 1536)
    hid_ref[...] = h_scr[mine, :]


def expert(x, w_gate, w_up, w_down):
    gate = dot(x, w_gate, 1, 0)
    up = dot(x, w_up, 1, 0)
    act = (gate / (1.0 + jnp.exp(-gate)) * up).astype(BF)
    return dot(act, w_down, 1, 0).astype(BF)


def near_kernel(x_ref, wg_ref, wu_ref, wd_ref, out_ref):
    x = jnp.concatenate([x_ref[:, i * CAP : (i + 1) * CAP, :].reshape(128, 1536) for i in range(2)], axis=0)
    y = expert(x, wg_ref[0], wu_ref[0], wd_ref[0])
    out_ref[...] = y.reshape(2, 8, CAP, 1536)


def far_kernel(place_ref, x_ref, w_ref, *refs):
    out_refs, (wg_scr, wu_scr, wd_scr, y_scr) = refs[0:8], refs[8:]
    me = place_ref[5]
    for z in range(8):
        wg_scr[z * 192 : (z + 1) * 192, :] = w_ref[z, 0:192, :]
        wu_scr[z * 192 : (z + 1) * 192, :] = w_ref[z, 192:384, :]
        for i in range(3):
            wd_scr[z * 64 : (z + 1) * 64, i * 512 : (i + 1) * 512] = w_ref[z, 384 + i * 64 : 448 + i * 64, :]
    y_scr[...] = expert(x_ref[...].reshape(128, 1536), wg_scr[...], wu_scr[...], wd_scr[...])
    for k in range(8):
        out_refs[k][...] = y_scr[pl.ds(pl.multiple_of((me + k) % 8 * CAP, CAP), CAP), :]


def close_kernel(place_ref, routes_ref, gates_ref, hid_ref, gain_ref, near_ref, *refs):
    far_refs, out_ref = refs[0:8], refs[8]
    lane = lax.broadcasted_iota(jnp.int32, (1, 640), 1)
    half, me, slot = place_ref[3], place_ref[5], lane // CAP
    near_of, far_of = (32 * half + slot) % EXPERTS, 32 - 8 * half + (me + 40 - slot) % 8
    expert_of = jnp.where(slot < 32, near_of, far_of).astype(F32)
    routed = routes_ref[...].astype(F32)
    hits, ranks = one_hot_rows(routed, expert_of, before_matrix(64))
    gate = jnp.zeros((64, 640), F32)
    for k in range(8):
        gate = gate + jnp.where(routed[:, k : k + 1] == expert_of, gates_ref[:, k : k + 1], 0.0)
    gate = jnp.where((ranks == (lane % CAP).astype(F32)) & (hits > 0.5), gate, 0.0)
    high = gate.astype(BF)
    low = (gate - high.astype(F32)).astype(BF)
    both = jnp.concatenate([high, low], axis=0)
    far = jnp.concatenate([ref[...] for ref in far_refs], axis=0)
    total = dot(both[:, 0:512], near_ref[...].reshape(512, 1536), 1, 0) + dot(both[:, 512:640], far, 1, 0)
    combined = hid_ref[...] + (total[0:64] + total[64:128])
    mean = jnp.sum(combined * combined, axis=1, keepdims=True) / 1536
    out = (combined * lax.rsqrt(mean + EPS) * gain_ref[...]).astype(BF)
    for z in range(8):
        out_ref[z] = out[:, z * 192 : (z + 1) * 192]


def smem():
    return pl.BlockSpec(memory_space=pltpu.SMEM)


def vmem():
    return pl.BlockSpec(memory_space=pltpu.VMEM)


def keep(value):
    return pltpu.with_memory_space_constraint(value, pltpu.VMEM)


def per_device(attn, resid, w_out, gain_mix, gain_out, routes, gates, w_gate, w_up, w_down):
    tp, h, y = lax.axis_index("tp"), lax.axis_index("h"), lax.axis_index("y")
    core, me = lax.axis_index("c"), lax.axis_index(("x", "c"))
    place = jnp.stack([core, h * 4 + y, y, h, tp, me])
    shape = jax.ShapeDtypeStruct
    my_routes = lax.dynamic_slice_in_dim(routes, tp * 64, 64, 0)
    my_gates = lax.dynamic_slice_in_dim(gates, tp * 64, 64, 0)

    send = pl.pallas_call(
        pack_kernel,
        out_shape=shape((8, 88, 384), BF),
        in_specs=[vmem()] * 3,
        out_specs=vmem(),
        compiler_params=params(),
        name="pack",
    )(attn.T, resid.T, w_out.T)
    got = lax.all_to_all(send, "tp", 0, 0, tiled=True)

    piece = pl.pallas_call(
        piece_kernel,
        grid_spec=pltpu.PrefetchScalarGridSpec(
            num_scalar_prefetch=1,
            grid=(1,),
            in_specs=[
                pl.BlockSpec((1, 192, 512), lambda i, p: (0, p[4], 0)),
                pl.BlockSpec((1, 192, 512), lambda i, p: (0, p[4], 0)),
                pl.BlockSpec((1, 64, 1536), lambda i, p: (0, p[4], 0)),
            ],
            out_specs=pl.BlockSpec((576, 512), lambda i, p: (0, 0)),
        ),
        out_shape=shape((576, 512), BF),
        compiler_params=params(),
        name="piece",
    )(place, w_gate, w_up, w_down)
    across = lambda v, a, b, c, d: lax.ppermute(v, ("h", "y"), [(a, b), (c, d)])
    step_1 = across(piece, 4, 3, 3, 4)
    step_3 = across(piece, 4, 1, 3, 6)
    got, step_1 = lax.optimization_barrier((got, step_1))

    tokens, w_y = pl.pallas_call(
        unpack_kernel,
        out_shape=(shape((64, 3200), BF), shape((8, 24, 1536), BF)),
        in_specs=[vmem()] * 2,
        out_specs=(vmem(), vmem()),
        compiler_params=params(),
        name="unpack",
    )(keep(got), my_routes)
    tokens = lax.all_gather(tokens, "y", axis=0, tiled=True)
    w_y = lax.all_to_all(w_y, ("h", "y"), 0, 0, tiled=True)
    w_x = lax.all_to_all(jnp.broadcast_to(w_y.reshape(1, 192, 1536), (4, 192, 1536)), "x", 0, 0, tiled=True)
    w_x, tokens, step_1, step_3 = lax.optimization_barrier((w_x, tokens, step_1, step_3))
    w_c = lax.ppermute(w_x, "c", [(0, 1), (1, 0)])
    step_2 = across(step_1, 3, 2, 4, 5)
    step_4 = across(step_3, 1, 0, 6, 7)

    send, hidden = pl.pallas_call(
        mix_kernel,
        out_shape=(shape((8, 80, 1536), BF), shape((64, 1536), F32)),
        in_specs=[smem()] + [vmem()] * 4,
        out_specs=(vmem(), vmem()),
        scratch_shapes=[pltpu.VMEM((1536, 1536), BF), pltpu.VMEM((256, 1536), F32), pltpu.VMEM((256, 1536), BF)],
        compiler_params=params(),
        name="mix",
    )(place, tokens, keep(w_x), w_c, gain_mix.reshape(1, 1536))
    step_2, step_4, _ = lax.optimization_barrier((step_2, step_4, send))
    far_piece = (step_1 + step_2) + (step_3 + step_4)
    far_weights = lax.all_gather(far_piece, "tp", axis=0, tiled=False)
    received = lax.all_to_all(send, ("x", "c"), 0, 0, tiled=True)

    whole = lambda *dims: pl.BlockSpec(dims, lambda i: (0,) * len(dims))
    near = pl.pallas_call(
        near_kernel,
        grid=(2,),
        out_shape=shape((4, 8, CAP, 1536), BF),
        in_specs=[
            pl.BlockSpec((8, 2 * CAP, 1536), lambda i: (0, i, 0)),
            whole(1, 1536, 512),
            whole(1, 1536, 512),
            whole(1, 512, 1536),
        ],
        out_specs=pl.BlockSpec((2, 8, CAP, 1536), lambda i: (i, 0, 0, 0)),
        compiler_params=params(),
        name="near",
    )(received, w_gate, w_up, w_down)
    near = lax.all_to_all(near.reshape(32, CAP, 1536), ("y", "x", "c"), 0, 0, tiled=True)
    far = pl.pallas_call(
        far_kernel,
        grid=(1,),
        out_shape=(shape((CAP, 1536), BF),) * 8,
        in_specs=[smem(), pl.BlockSpec((8, CAP, 1536), lambda i: (0, 4, 0))] + [whole(8, 576, 512)],
        out_specs=(whole(CAP, 1536),) * 8,
        scratch_shapes=[
            pltpu.VMEM((1536, 512), BF),
            pltpu.VMEM((1536, 512), BF),
            pltpu.VMEM((512, 1536), BF),
            pltpu.VMEM((128, 1536), BF),
        ],
        compiler_params=params(),
        name="far",
    )(place, received, far_weights)
    far = [far[0]] + [lax.ppermute(far[k], ("x", "c"), [(i, (i + k) % 8) for i in range(8)]) for k in range(1, 8)]

    finished = pl.pallas_call(
        close_kernel,
        out_shape=shape((8, 64, 192), BF),
        in_specs=[smem()] + [vmem()] * 13,
        out_specs=vmem(),
        compiler_params=params(),
        name="close",
    )(place, my_routes, my_gates, hidden, gain_out.reshape(1, 1536), keep(near), *far)
    return lax.all_to_all(finished, "tp", 0, 0, tiled=True).reshape(512, 192)


def solution(mesh):
    fine = Mesh(mesh.devices.reshape(8, 2, 4, 4, 2), ("tp",) + EP)
    return jax.shard_map(
        per_device,
        mesh=fine,
        in_specs=(
            P(EP, "tp"),
            P(EP, "tp"),
            P("tp", EP),
            P(),
            P(),
            P(EP, None),
            P(EP, None),
            P(EP, None, None),
            P(EP, None, None),
            P(EP, None, None),
        ),
        out_specs=P(EP, "tp"),
        check_vma=False,
    )
```

```python
import jax
import jax.numpy as jnp
from jax import lax
from jax.experimental import pallas as pl
from jax.experimental.pallas import tpu as pltpu
from jax.sharding import Mesh, PartitionSpec as P

EXPERTS = 40
CAP = 16
EPS = 1e-05
BF = jnp.bfloat16
F32 = jnp.float32
EP = ("h", "y", "x", "c")
VMEM = 56 * 1024 * 1024


def params():
    return pltpu.CompilerParams(vmem_limit_bytes=VMEM)


def dot(a, b, ca, cb):
    return lax.dot_general(a, b, (((ca,), (cb,)), ((), ())), preferred_element_type=F32)


def project_kernel(place_ref, attn_ref, resid_ref, w_ref, out_ref):
    tp = place_ref[4]
    weights = w_ref[...].reshape(1536, 192)
    at = lax.broadcasted_iota(jnp.int32, (1536, 192), 0)
    of = lax.broadcasted_iota(jnp.int32, (1536, 192), 1)
    choose = jnp.where(at == of + tp * 192, 1.0, 0.0).astype(BF)
    part = dot(attn_ref[...].T, weights, 1, 1) + dot(resid_ref[...].T, choose, 1, 1)
    out_ref[...] = part.astype(BF).reshape(8, 64, 1536)


def piece_kernel(place_ref, wg_ref, wu_ref, wd_ref, out_ref):
    out_ref[0:192, :] = wg_ref[0]
    out_ref[192:384, :] = wu_ref[0]
    for i in range(3):
        out_ref[384 + i * 64 : 448 + i * 64, :] = wd_ref[0, :, i * 512 : (i + 1) * 512]


def one_hot_rows(routed, expert, rank_of):
    hits = jnp.zeros((routed.shape[0], expert.shape[1]), F32)
    for k in range(8):
        hits = hits + jnp.where(routed[:, k : k + 1] == expert, 1.0, 0.0)
    ranks = dot(rank_of, hits.astype(BF), 1, 0)
    return hits, ranks


def before_matrix(rows):
    a = lax.broadcasted_iota(jnp.int32, (rows, rows), 0)
    b = lax.broadcasted_iota(jnp.int32, (rows, rows), 1)
    keep = (b < a) & (a // 64 == b // 64)
    return jnp.where(keep, 1.0, 0.0).astype(BF)


def lane_experts(place_ref, lane):
    half, me = place_ref[3], place_ref[5]
    slot = lane // CAP
    near = (32 * half + slot) % EXPERTS
    far = 32 - 8 * half + (me + slot) % 8
    return jnp.where(slot < 32, near, far).astype(F32)


def mix_kernel(place_ref, part_ref, routes_ref, gain_ref, send_ref, hid_ref, *far_refs):
    hidden = part_ref[0].astype(F32)
    for z in range(1, 8):
        hidden = hidden + part_ref[z].astype(F32)
    hid_ref[...] = hidden
    mean = jnp.sum(hidden * hidden, axis=1, keepdims=True) / 1536
    normed = (hidden * lax.rsqrt(mean + EPS) * gain_ref[...]).astype(BF)
    lane = lax.broadcasted_iota(jnp.int32, (1, 640), 1)
    hits, ranks = one_hot_rows(routes_ref[...].astype(F32), lane_experts(place_ref, lane), before_matrix(64))
    pick = jnp.where(ranks == (lane % CAP).astype(F32), hits, 0.0).astype(BF)
    far = dot(pick[:, 512:640], normed, 0, 0).astype(BF)
    for k in range(8):
        far_refs[k][...] = far[k * CAP : (k + 1) * CAP]
    send_ref[...] = dot(pick[:, 0:512], normed, 0, 0).astype(BF).reshape(32, CAP, 1536)


def expert(x, w_gate, w_up, w_down):
    gate = dot(x, w_gate, 1, 0)
    up = dot(x, w_up, 1, 0)
    act = (gate / (1.0 + jnp.exp(-gate)) * up).astype(BF)
    return dot(act, w_down, 1, 0).astype(BF)


def near_kernel(x_ref, wg_ref, wu_ref, wd_ref, out_ref):
    y = expert(x_ref[...].reshape(256, 1536), wg_ref[0], wu_ref[0], wd_ref[0])
    out_ref[...] = y.reshape(16, CAP, 1536)


def far_kernel(*refs):
    x_refs, w_ref, out_refs, (wg_scr, wu_scr, wd_scr) = refs[0:8], refs[8], refs[9:17], refs[17:]
    for z in range(8):
        wg_scr[z * 192 : (z + 1) * 192, :] = w_ref[z, 0:192, :]
        wu_scr[z * 192 : (z + 1) * 192, :] = w_ref[z, 192:384, :]
        for i in range(3):
            wd_scr[z * 64 : (z + 1) * 64, i * 512 : (i + 1) * 512] = w_ref[z, 384 + i * 64 : 448 + i * 64, :]
    x = jnp.concatenate([ref[...] for ref in x_refs], axis=0)
    y = expert(x, wg_scr[...], wu_scr[...], wd_scr[...])
    for k in range(8):
        out_refs[k][...] = y[k * CAP : (k + 1) * CAP]


def close_kernel(place_ref, routes_ref, gates_ref, hid_ref, gain_ref, near_ref, *refs):
    far_refs, out_ref = refs[0:8], refs[8]
    lane = lax.broadcasted_iota(jnp.int32, (1, 640), 1)
    expert_of = lane_experts(place_ref, lane)
    routed = routes_ref[...].astype(F32)
    hits, ranks = one_hot_rows(routed, expert_of, before_matrix(64))
    gate = jnp.zeros((64, 640), F32)
    for k in range(8):
        gate = gate + jnp.where(routed[:, k : k + 1] == expert_of, gates_ref[:, k : k + 1], 0.0)
    gate = jnp.where((ranks == (lane % CAP).astype(F32)) & (hits > 0.5), gate, 0.0)
    high = gate.astype(BF)
    low = (gate - high.astype(F32)).astype(BF)
    both = jnp.concatenate([high, low], axis=0)
    far = jnp.concatenate([ref[...] for ref in far_refs], axis=0)
    total = dot(both[:, 0:512], near_ref[...].reshape(512, 1536), 1, 0) + dot(both[:, 512:640], far, 1, 0)
    combined = hid_ref[...] + (total[0:64] + total[64:128])
    mean = jnp.sum(combined * combined, axis=1, keepdims=True) / 1536
    out = (combined * lax.rsqrt(mean + EPS) * gain_ref[...]).astype(BF)
    for z in range(8):
        out_ref[z] = out[:, z * 192 : (z + 1) * 192]


def smem():
    return pl.BlockSpec(memory_space=pltpu.SMEM)


def vmem():
    return pl.BlockSpec(memory_space=pltpu.VMEM)


def keep(value):
    return pltpu.with_memory_space_constraint(value, pltpu.VMEM)


def per_device(attn, resid, w_out, gain_mix, gain_out, routes, gates, w_gate, w_up, w_down):
    tp, h, y = lax.axis_index("tp"), lax.axis_index("h"), lax.axis_index("y")
    core, me = lax.axis_index("c"), lax.axis_index(("x", "c"))
    place = jnp.stack([core, h * 4 + y, y, h, tp, me])
    shape = jax.ShapeDtypeStruct
    my_routes = lax.dynamic_slice_in_dim(routes, tp * 64, 64, 0)
    my_gates = lax.dynamic_slice_in_dim(gates, tp * 64, 64, 0)

    piece = pl.pallas_call(
        piece_kernel,
        grid_spec=pltpu.PrefetchScalarGridSpec(
            num_scalar_prefetch=1,
            grid=(1,),
            in_specs=[
                pl.BlockSpec((1, 192, 512), lambda i, p: (0, p[4], 0)),
                pl.BlockSpec((1, 192, 512), lambda i, p: (0, p[4], 0)),
                pl.BlockSpec((1, 64, 1536), lambda i, p: (0, p[4], 0)),
            ],
            out_specs=pl.BlockSpec((576, 512), lambda i, p: (0, 0)),
        ),
        out_shape=shape((576, 512), BF),
        compiler_params=params(),
        name="piece",
    )(place, w_gate, w_up, w_down)
    across = lambda v, a, b, c, d: lax.ppermute(v, ("h", "y"), [(a, b), (c, d)])
    step_1 = across(piece, 4, 3, 3, 4)
    step_3 = across(piece, 4, 1, 3, 6)
    columns = lax.all_to_all(jnp.broadcast_to(w_out.T[None], (64, 24, 192)), EP, 0, 0, tiled=True)
    columns, step_1, step_3 = lax.optimization_barrier((columns, step_1, step_3))
    step_2 = across(step_1, 3, 2, 4, 5)
    step_4 = across(step_3, 1, 0, 6, 7)

    parts = pl.pallas_call(
        project_kernel,
        out_shape=shape((8, 64, 1536), BF),
        in_specs=[smem()] + [vmem()] * 3,
        out_specs=vmem(),
        compiler_params=params(),
        name="project",
    )(place, attn.T, resid.T, keep(columns))
    parts = lax.all_to_all(parts, "tp", 0, 0, tiled=True)
    far_piece = (step_1 + step_2) + (step_3 + step_4)
    parts, far_piece = lax.optimization_barrier((parts, far_piece))
    far_weights = lax.all_gather(far_piece, "tp", axis=0, tiled=False)

    rows = shape((CAP, 1536), BF)
    send, hidden, *far = pl.pallas_call(
        mix_kernel,
        out_shape=(shape((32, CAP, 1536), BF), shape((64, 1536), F32)) + (rows,) * 8,
        in_specs=[smem()] + [vmem()] * 3,
        out_specs=(vmem(),) * 10,
        compiler_params=params(),
        name="mix",
    )(place, keep(parts), my_routes, gain_mix.reshape(1, 1536))

    shift = lambda v, k: lax.ppermute(v, ("x", "c"), [(i, (i + k) % 8) for i in range(8)])
    far = far[0:1] + [shift(far[k], k) for k in range(1, 8)]
    received = lax.all_to_all(send, ("y", "x", "c"), 0, 0, tiled=True)
    received, far = lax.optimization_barrier((received, far))

    whole = lambda *dims: pl.BlockSpec(dims, lambda i: (0,) * len(dims))
    near = pl.pallas_call(
        near_kernel,
        grid=(2,),
        out_shape=shape((32, CAP, 1536), BF),
        in_specs=[
            pl.BlockSpec((16, CAP, 1536), lambda i: (i, 0, 0)),
            whole(1, 1536, 512),
            whole(1, 1536, 512),
            whole(1, 512, 1536),
        ],
        out_specs=pl.BlockSpec((16, CAP, 1536), lambda i: (i, 0, 0)),
        compiler_params=params(),
        name="near",
    )(received, w_gate, w_up, w_down)
    far = pl.pallas_call(
        far_kernel,
        out_shape=(rows,) * 8,
        in_specs=[vmem()] * 9,
        out_specs=(vmem(),) * 8,
        scratch_shapes=[pltpu.VMEM((1536, 512), BF), pltpu.VMEM((1536, 512), BF), pltpu.VMEM((512, 1536), BF)],
        compiler_params=params(),
        name="far",
    )(*far, far_weights)
    near = lax.all_to_all(near, ("y", "x", "c"), 0, 0, tiled=True)
    far = [far[0]] + [shift(far[k], 8 - k) for k in range(1, 8)]

    finished = pl.pallas_call(
        close_kernel,
        out_shape=shape((8, 64, 192), BF),
        in_specs=[smem()] + [vmem()] * 13,
        out_specs=vmem(),
        compiler_params=params(),
        name="close",
    )(place, my_routes, my_gates, hidden, gain_out.reshape(1, 1536), keep(near), *far)
    return lax.all_to_all(finished, "tp", 0, 0, tiled=True).reshape(512, 192)


def solution(mesh):
    fine = Mesh(mesh.devices.reshape(8, 2, 4, 4, 2), ("tp",) + EP)
    return jax.shard_map(
        per_device,
        mesh=fine,
        in_specs=(
            P(EP, "tp"),
            P(EP, "tp"),
            P("tp", EP),
            P(),
            P(),
            P(EP, None),
            P(EP, None),
            P(EP, None, None),
            P(EP, None, None),
            P(EP, None, None),
        ),
        out_specs=P(EP, "tp"),
        check_vma=False,
    )
```

```python
import jax
import jax.numpy as jnp
from jax import lax
from jax.experimental import pallas as pl
from jax.experimental.pallas import tpu as pltpu
from jax.sharding import Mesh, PartitionSpec as P

EXPERTS = 40
CAP = 16
EPS = 1e-05
BF = jnp.bfloat16
F32 = jnp.float32
EP = ("h", "y", "x", "c")
VMEM = 56 * 1024 * 1024


def params():
    return pltpu.CompilerParams(vmem_limit_bytes=VMEM)


def dot(a, b, ca, cb):
    return lax.dot_general(a, b, (((ca,), (cb,)), ((), ())), preferred_element_type=F32)


def project_kernel(place_ref, attn_ref, resid_ref, w_ref, out_ref):
    tp = place_ref[4]
    weights = w_ref[...].reshape(1536, 192)
    at = lax.broadcasted_iota(jnp.int32, (1536, 192), 0)
    of = lax.broadcasted_iota(jnp.int32, (1536, 192), 1)
    choose = jnp.where(at == of + tp * 192, 1.0, 0.0).astype(BF)
    part = dot(attn_ref[...].T, weights, 1, 1) + dot(resid_ref[...].T, choose, 1, 1)
    out_ref[...] = part.astype(BF).reshape(8, 64, 1536)


def piece_kernel(place_ref, wg_ref, wu_ref, wd_ref, out_ref):
    out_ref[0:192, :] = wg_ref[0]
    out_ref[192:384, :] = wu_ref[0]
    for i in range(3):
        out_ref[384 + i * 64 : 448 + i * 64, :] = wd_ref[0, :, i * 512 : (i + 1) * 512]


def one_hot_rows(routed, expert, rank_of):
    hits = jnp.zeros((routed.shape[0], expert.shape[1]), F32)
    for k in range(8):
        hits = hits + jnp.where(routed[:, k : k + 1] == expert, 1.0, 0.0)
    ranks = dot(rank_of, hits.astype(BF), 1, 0)
    return hits, ranks


def before_matrix(rows):
    a = lax.broadcasted_iota(jnp.int32, (rows, rows), 0)
    b = lax.broadcasted_iota(jnp.int32, (rows, rows), 1)
    keep = (b < a) & (a // 64 == b // 64)
    return jnp.where(keep, 1.0, 0.0).astype(BF)


def lane_experts(place_ref, lane):
    half, me = place_ref[3], place_ref[5]
    slot = lane // CAP
    near = (32 * half + slot) % EXPERTS
    far = 32 - 8 * half + (me + slot) % 8
    return jnp.where(slot < 32, near, far).astype(F32)


def mix_kernel(place_ref, part_ref, routes_ref, gain_ref, send_ref, hid_ref, *far_refs):
    hidden = part_ref[0].astype(F32)
    for z in range(1, 8):
        hidden = hidden + part_ref[z].astype(F32)
    hid_ref[...] = hidden
    mean = jnp.sum(hidden * hidden, axis=1, keepdims=True) / 1536
    normed = (hidden * lax.rsqrt(mean + EPS) * gain_ref[...]).astype(BF)
    lane = lax.broadcasted_iota(jnp.int32, (1, 640), 1)
    hits, ranks = one_hot_rows(routes_ref[...].astype(F32), lane_experts(place_ref, lane), before_matrix(64))
    pick = jnp.where(ranks == (lane % CAP).astype(F32), hits, 0.0).astype(BF)
    far = dot(pick[:, 512:640], normed, 0, 0).astype(BF)
    for k in range(8):
        far_refs[k][...] = far[k * CAP : (k + 1) * CAP]
    send_ref[...] = dot(pick[:, 0:512], normed, 0, 0).astype(BF).reshape(32, CAP, 1536)


def expert(x, w_gate, w_up, w_down):
    gate = dot(x, w_gate, 1, 0)
    up = dot(x, w_up, 1, 0)
    act = (gate / (1.0 + jnp.exp(-gate)) * up).astype(BF)
    return dot(act, w_down, 1, 0).astype(BF)


def near_kernel(x_ref, wg_ref, wu_ref, wd_ref, out_ref):
    y = expert(x_ref[...].reshape(256, 1536), wg_ref[0], wu_ref[0], wd_ref[0])
    out_ref[...] = y.reshape(16, CAP, 1536)


def far_kernel(*refs):
    x_refs, w_ref, out_refs, (wg_scr, wu_scr, wd_scr) = refs[0:8], refs[8], refs[9:17], refs[17:]
    for z in range(8):
        wg_scr[z * 192 : (z + 1) * 192, :] = w_ref[z, 0:192, :]
        wu_scr[z * 192 : (z + 1) * 192, :] = w_ref[z, 192:384, :]
        for i in range(3):
            wd_scr[z * 64 : (z + 1) * 64, i * 512 : (i + 1) * 512] = w_ref[z, 384 + i * 64 : 448 + i * 64, :]
    x = jnp.concatenate([ref[...] for ref in x_refs], axis=0)
    y = expert(x, wg_scr[...], wu_scr[...], wd_scr[...])
    for k in range(8):
        out_refs[k][...] = y[k * CAP : (k + 1) * CAP]


def close_kernel(place_ref, routes_ref, gates_ref, hid_ref, gain_ref, near_ref, *refs):
    far_refs, out_ref = refs[0:8], refs[8]
    lane = lax.broadcasted_iota(jnp.int32, (1, 640), 1)
    expert_of = lane_experts(place_ref, lane)
    routed = routes_ref[...].astype(F32)
    hits, ranks = one_hot_rows(routed, expert_of, before_matrix(64))
    gate = jnp.zeros((64, 640), F32)
    for k in range(8):
        gate = gate + jnp.where(routed[:, k : k + 1] == expert_of, gates_ref[:, k : k + 1], 0.0)
    gate = jnp.where((ranks == (lane % CAP).astype(F32)) & (hits > 0.5), gate, 0.0)
    high = gate.astype(BF)
    low = (gate - high.astype(F32)).astype(BF)
    both = jnp.concatenate([high, low], axis=0)
    far = jnp.concatenate([ref[...] for ref in far_refs], axis=0)
    total = dot(both[:, 0:512], near_ref[...].reshape(512, 1536), 1, 0) + dot(both[:, 512:640], far, 1, 0)
    combined = hid_ref[...] + (total[0:64] + total[64:128])
    mean = jnp.sum(combined * combined, axis=1, keepdims=True) / 1536
    out = (combined * lax.rsqrt(mean + EPS) * gain_ref[...]).astype(BF)
    for z in range(8):
        out_ref[z] = out[:, z * 192 : (z + 1) * 192]


def smem():
    return pl.BlockSpec(memory_space=pltpu.SMEM)


def vmem():
    return pl.BlockSpec(memory_space=pltpu.VMEM)


def keep(value):
    return pltpu.with_memory_space_constraint(value, pltpu.VMEM)


def per_device(attn, resid, w_out, gain_mix, gain_out, routes, gates, w_gate, w_up, w_down):
    tp, h, y = lax.axis_index("tp"), lax.axis_index("h"), lax.axis_index("y")
    core, me = lax.axis_index("c"), lax.axis_index(("x", "c"))
    place = jnp.stack([core, h * 4 + y, y, h, tp, me])
    shape = jax.ShapeDtypeStruct
    my_routes = lax.dynamic_slice_in_dim(routes, tp * 64, 64, 0)
    my_gates = lax.dynamic_slice_in_dim(gates, tp * 64, 64, 0)

    piece = pl.pallas_call(
        piece_kernel,
        grid_spec=pltpu.PrefetchScalarGridSpec(
            num_scalar_prefetch=1,
            grid=(1,),
            in_specs=[
                pl.BlockSpec((1, 192, 512), lambda i, p: (0, p[4], 0)),
                pl.BlockSpec((1, 192, 512), lambda i, p: (0, p[4], 0)),
                pl.BlockSpec((1, 64, 1536), lambda i, p: (0, p[4], 0)),
            ],
            out_specs=pl.BlockSpec((576, 512), lambda i, p: (0, 0)),
        ),
        out_shape=shape((576, 512), BF),
        compiler_params=params(),
        name="piece",
    )(place, w_gate, w_up, w_down)
    crossed = lax.ppermute(piece, ("h", "y"), [(4, 3), (3, 4)])
    columns = lax.all_to_all(jnp.broadcast_to(w_out.T[None], (64, 24, 192)), EP, 0, 0, tiled=True)
    pieces = lax.all_gather(crossed, "y", axis=0, tiled=False)

    parts = pl.pallas_call(
        project_kernel,
        out_shape=shape((8, 64, 1536), BF),
        in_specs=[smem()] + [vmem()] * 3,
        out_specs=vmem(),
        compiler_params=params(),
        name="project",
    )(place, attn.T, resid.T, keep(columns))
    parts = lax.all_to_all(parts, "tp", 0, 0, tiled=True)
    rows = shape((CAP, 1536), BF)
    send, hidden, *far = pl.pallas_call(
        mix_kernel,
        out_shape=(shape((32, CAP, 1536), BF), shape((64, 1536), F32)) + (rows,) * 8,
        in_specs=[smem()] + [vmem()] * 3,
        out_specs=(vmem(),) * 10,
        compiler_params=params(),
        name="mix",
    )(place, keep(parts), my_routes, gain_mix.reshape(1, 1536))

    pieces, _ = lax.optimization_barrier((pieces, send))
    far_piece = lax.dynamic_index_in_dim(pieces, 3 - 3 * h, 0, keepdims=False)
    far_weights = lax.all_gather(far_piece, "tp", axis=0, tiled=False)

    shift = lambda v, k: lax.ppermute(v, ("x", "c"), [(i, (i + k) % 8) for i in range(8)])
    far = far[0:1] + [shift(far[k], k) for k in range(1, 8)]
    received = lax.all_to_all(send, ("y", "x", "c"), 0, 0, tiled=True)
    received, far = lax.optimization_barrier((received, far))

    whole = lambda *dims: pl.BlockSpec(dims, lambda i: (0,) * len(dims))
    near = pl.pallas_call(
        near_kernel,
        grid=(2,),
        out_shape=shape((32, CAP, 1536), BF),
        in_specs=[
            pl.BlockSpec((16, CAP, 1536), lambda i: (i, 0, 0)),
            whole(1, 1536, 512),
            whole(1, 1536, 512),
            whole(1, 512, 1536),
        ],
        out_specs=pl.BlockSpec((16, CAP, 1536), lambda i: (i, 0, 0)),
        compiler_params=params(),
        name="near",
    )(received, w_gate, w_up, w_down)
    far = pl.pallas_call(
        far_kernel,
        out_shape=(rows,) * 8,
        in_specs=[vmem()] * 9,
        out_specs=(vmem(),) * 8,
        scratch_shapes=[pltpu.VMEM((1536, 512), BF), pltpu.VMEM((1536, 512), BF), pltpu.VMEM((512, 1536), BF)],
        compiler_params=params(),
        name="far",
    )(*far, far_weights)
    near = lax.all_to_all(near, ("y", "x", "c"), 0, 0, tiled=True)
    far = [far[0]] + [shift(far[k], 8 - k) for k in range(1, 8)]

    finished = pl.pallas_call(
        close_kernel,
        out_shape=shape((8, 64, 192), BF),
        in_specs=[smem()] + [vmem()] * 13,
        out_specs=vmem(),
        compiler_params=params(),
        name="close",
    )(place, my_routes, my_gates, hidden, gain_out.reshape(1, 1536), keep(near), *far)
    return lax.all_to_all(finished, "tp", 0, 0, tiled=True).reshape(512, 192)


def solution(mesh):
    fine = Mesh(mesh.devices.reshape(8, 2, 4, 4, 2), ("tp",) + EP)
    return jax.shard_map(
        per_device,
        mesh=fine,
        in_specs=(
            P(EP, "tp"),
            P(EP, "tp"),
            P("tp", EP),
            P(),
            P(),
            P(EP, None),
            P(EP, None),
            P(EP, None, None),
            P(EP, None, None),
            P(EP, None, None),
        ),
        out_specs=P(EP, "tp"),
        check_vma=False,
    )
```

```python
import jax
import jax.numpy as jnp
from jax import lax
from jax.experimental import pallas as pl
from jax.experimental.pallas import tpu as pltpu
from jax.sharding import Mesh, PartitionSpec as P

EXPERTS = 40
CAP = 16
EPS = 1e-05
BF = jnp.bfloat16
F32 = jnp.float32
EP = ("h", "y", "x", "c")
VMEM = 56 * 1024 * 1024


def params():
    return pltpu.CompilerParams(vmem_limit_bytes=VMEM)


def dot(a, b, ca, cb):
    return lax.dot_general(a, b, (((ca,), (cb,)), ((), ())), preferred_element_type=F32)


def project_kernel(place_ref, attn_ref, resid_ref, w_ref, out_ref):
    tp = place_ref[4]
    weights = w_ref[...].reshape(1536, 192)
    at = lax.broadcasted_iota(jnp.int32, (1536, 192), 0)
    of = lax.broadcasted_iota(jnp.int32, (1536, 192), 1)
    choose = jnp.where(at == of + tp * 192, 1.0, 0.0).astype(BF)
    part = dot(attn_ref[...].T, weights, 1, 1) + dot(resid_ref[...].T, choose, 1, 1)
    out_ref[...] = part.astype(BF).reshape(8, 64, 1536)


def piece_kernel(place_ref, wg_ref, wu_ref, wd_ref, out_ref, sems):
    tp = place_ref[4]
    wide, thin = pl.ds(pl.multiple_of(tp * 192, 64), 192), pl.ds(pl.multiple_of(tp * 64, 64), 64)
    moves = [(wg_ref.at[0, wide, :], 0, 192), (wu_ref.at[0, wide, :], 192, 192)]
    moves += [(wd_ref.at[0, thin, i * 512 : (i + 1) * 512], 384 + i * 64, 64) for i in range(3)]
    copies = [
        pltpu.make_async_copy(source, out_ref.at[at : at + count, :], sems.at[i])
        for i, (source, at, count) in enumerate(moves)
    ]
    for copy in copies:
        copy.start()
    for copy in copies:
        copy.wait()


def choose_kernel(place_ref, pieces_ref, out_ref, sems):
    from_row = 3 - 3 * place_ref[3]
    copies = [
        pltpu.make_async_copy(
            pieces_ref.at[from_row, i * 144 : (i + 1) * 144, :], out_ref.at[i * 144 : (i + 1) * 144, :], sems.at[i]
        )
        for i in range(4)
    ]
    for copy in copies:
        copy.start()
    for copy in copies:
        copy.wait()


def one_hot_rows(routed, expert, rank_of):
    hits = jnp.zeros((routed.shape[0], expert.shape[1]), F32)
    for k in range(8):
        hits = hits + jnp.where(routed[:, k : k + 1] == expert, 1.0, 0.0)
    ranks = dot(rank_of, hits.astype(BF), 1, 0)
    return hits, ranks


def before_matrix(rows):
    a = lax.broadcasted_iota(jnp.int32, (rows, rows), 0)
    b = lax.broadcasted_iota(jnp.int32, (rows, rows), 1)
    keep = (b < a) & (a // 64 == b // 64)
    return jnp.where(keep, 1.0, 0.0).astype(BF)


def lane_experts(place_ref, lane):
    half, me = place_ref[3], place_ref[5]
    slot = lane // CAP
    near = (32 * half + slot) % EXPERTS
    far = 32 - 8 * half + (me + slot) % 8
    return jnp.where(slot < 32, near, far).astype(F32)


def mix_kernel(place_ref, part_ref, routes_ref, gain_ref, send_ref, hid_ref, *far_refs):
    hidden = part_ref[0].astype(F32)
    for z in range(1, 8):
        hidden = hidden + part_ref[z].astype(F32)
    hid_ref[...] = hidden
    mean = jnp.sum(hidden * hidden, axis=1, keepdims=True) / 1536
    normed = (hidden * lax.rsqrt(mean + EPS) * gain_ref[...]).astype(BF)
    lane = lax.broadcasted_iota(jnp.int32, (1, 640), 1)
    hits, ranks = one_hot_rows(routes_ref[...].astype(F32), lane_experts(place_ref, lane), before_matrix(64))
    pick = jnp.where(ranks == (lane % CAP).astype(F32), hits, 0.0).astype(BF)
    far = dot(pick[:, 512:640], normed, 0, 0).astype(BF)
    for k in range(8):
        far_refs[k][...] = far[k * CAP : (k + 1) * CAP]
    send_ref[...] = dot(pick[:, 0:512], normed, 0, 0).astype(BF).reshape(32, CAP, 1536)


def expert(x, w_gate, w_up, w_down):
    gate = dot(x, w_gate, 1, 0)
    up = dot(x, w_up, 1, 0)
    act = (gate / (1.0 + jnp.exp(-gate)) * up).astype(BF)
    return dot(act, w_down, 1, 0).astype(BF)


def near_kernel(x_ref, wg_ref, wu_ref, wd_ref, out_ref):
    half = pl.ds(pl.program_id(0) * 16, 16)
    y = expert(x_ref[half].reshape(256, 1536), wg_ref[0], wu_ref[0], wd_ref[0])
    out_ref[...] = y.reshape(16, CAP, 1536)


def far_kernel(*refs):
    x_refs, w_ref, out_refs, (wg_scr, wu_scr, wd_scr) = refs[0:8], refs[8], refs[9:17], refs[17:]
    for z in range(8):
        wg_scr[z * 192 : (z + 1) * 192, :] = w_ref[z, 0:192, :]
        wu_scr[z * 192 : (z + 1) * 192, :] = w_ref[z, 192:384, :]
        for i in range(3):
            wd_scr[z * 64 : (z + 1) * 64, i * 512 : (i + 1) * 512] = w_ref[z, 384 + i * 64 : 448 + i * 64, :]
    x = jnp.concatenate([ref[...] for ref in x_refs], axis=0)
    y = expert(x, wg_scr[...], wu_scr[...], wd_scr[...])
    for k in range(8):
        out_refs[k][...] = y[k * CAP : (k + 1) * CAP]


def close_kernel(place_ref, routes_ref, gates_ref, hid_ref, gain_ref, near_ref, *refs):
    far_refs, out_ref = refs[0:8], refs[8]
    lane = lax.broadcasted_iota(jnp.int32, (1, 640), 1)
    expert_of = lane_experts(place_ref, lane)
    routed = routes_ref[...].astype(F32)
    hits, ranks = one_hot_rows(routed, expert_of, before_matrix(64))
    gate = jnp.zeros((64, 640), F32)
    for k in range(8):
        gate = gate + jnp.where(routed[:, k : k + 1] == expert_of, gates_ref[:, k : k + 1], 0.0)
    gate = jnp.where((ranks == (lane % CAP).astype(F32)) & (hits > 0.5), gate, 0.0)
    high = gate.astype(BF)
    low = (gate - high.astype(F32)).astype(BF)
    both = jnp.concatenate([high, low], axis=0)
    far = jnp.concatenate([ref[...] for ref in far_refs], axis=0)
    total = dot(both[:, 0:512], near_ref[...].reshape(512, 1536), 1, 0) + dot(both[:, 512:640], far, 1, 0)
    combined = hid_ref[...] + (total[0:64] + total[64:128])
    mean = jnp.sum(combined * combined, axis=1, keepdims=True) / 1536
    out = (combined * lax.rsqrt(mean + EPS) * gain_ref[...]).astype(BF)
    for z in range(8):
        out_ref[z] = out[:, z * 192 : (z + 1) * 192]


def smem():
    return pl.BlockSpec(memory_space=pltpu.SMEM)


def vmem():
    return pl.BlockSpec(memory_space=pltpu.VMEM)


def keep(value):
    return pltpu.with_memory_space_constraint(value, pltpu.VMEM)


def per_device(attn, resid, w_out, gain_mix, gain_out, routes, gates, w_gate, w_up, w_down):
    tp, h, y = lax.axis_index("tp"), lax.axis_index("h"), lax.axis_index("y")
    core, me = lax.axis_index("c"), lax.axis_index(("x", "c"))
    place = jnp.stack([core, h * 4 + y, y, h, tp, me])
    shape = jax.ShapeDtypeStruct
    my_routes = lax.dynamic_slice_in_dim(routes, tp * 64, 64, 0)
    my_gates = lax.dynamic_slice_in_dim(gates, tp * 64, 64, 0)

    anywhere = pl.BlockSpec(memory_space=pltpu.HBM)
    piece = pl.pallas_call(
        piece_kernel,
        out_shape=shape((576, 512), BF),
        in_specs=[smem()] + [anywhere] * 3,
        out_specs=anywhere,
        scratch_shapes=[pltpu.SemaphoreType.DMA((5,))],
        compiler_params=params(),
        name="piece",
    )(place, w_gate, w_up, w_down)
    crossed = lax.ppermute(piece, ("h", "y"), [(4, 3), (3, 4)])
    columns = lax.all_to_all(jnp.broadcast_to(w_out.T[None], (64, 24, 192)), EP, 0, 0, tiled=True)
    pieces = lax.all_gather(crossed, "y", axis=0, tiled=False)

    parts = pl.pallas_call(
        project_kernel,
        out_shape=shape((8, 64, 1536), BF),
        in_specs=[smem()] + [vmem()] * 3,
        out_specs=vmem(),
        compiler_params=params(),
        name="project",
    )(place, attn.T, resid.T, keep(columns))
    parts = lax.all_to_all(parts, "tp", 0, 0, tiled=True)
    rows = shape((CAP, 1536), BF)
    send, hidden, *far = pl.pallas_call(
        mix_kernel,
        out_shape=(shape((32, CAP, 1536), BF), shape((64, 1536), F32)) + (rows,) * 8,
        in_specs=[smem()] + [vmem()] * 3,
        out_specs=(vmem(),) * 10,
        compiler_params=params(),
        name="mix",
    )(place, keep(parts), my_routes, gain_mix.reshape(1, 1536))

    pieces, _ = lax.optimization_barrier((pieces, send))
    far_piece = pl.pallas_call(
        choose_kernel,
        out_shape=shape((576, 512), BF),
        in_specs=[smem(), anywhere],
        out_specs=anywhere,
        scratch_shapes=[pltpu.SemaphoreType.DMA((4,))],
        compiler_params=params(),
        name="choose",
    )(place, pieces)
    far_weights = lax.all_gather(far_piece, "tp", axis=0, tiled=False)

    shift = lambda v, k: lax.ppermute(v, ("x", "c"), [(i, (i + k) % 8) for i in range(8)])
    far = far[0:1] + [shift(far[k], k) for k in range(1, 8)]
    received = lax.all_to_all(send, ("y", "x", "c"), 0, 0, tiled=True)
    received, far = lax.optimization_barrier((received, far))

    near = pl.pallas_call(
        near_kernel,
        grid=(2,),
        out_shape=shape((32, CAP, 1536), BF),
        in_specs=[vmem()] * 4,
        out_specs=pl.BlockSpec((16, CAP, 1536), lambda i: (i, 0, 0)),
        compiler_params=pltpu.CompilerParams(vmem_limit_bytes=40 * 1024 * 1024),
        name="near",
    )(keep(received), keep(w_gate), w_up, w_down)
    far = pl.pallas_call(
        far_kernel,
        out_shape=(rows,) * 8,
        in_specs=[vmem()] * 9,
        out_specs=(vmem(),) * 8,
        scratch_shapes=[pltpu.VMEM((1536, 512), BF), pltpu.VMEM((1536, 512), BF), pltpu.VMEM((512, 1536), BF)],
        compiler_params=params(),
        name="far",
    )(*far, far_weights)
    near = lax.all_to_all(near, ("y", "x", "c"), 0, 0, tiled=True)
    far = [far[0]] + [shift(far[k], 8 - k) for k in range(1, 8)]

    finished = pl.pallas_call(
        close_kernel,
        out_shape=shape((8, 64, 192), BF),
        in_specs=[smem()] + [vmem()] * 13,
        out_specs=vmem(),
        compiler_params=params(),
        name="close",
    )(place, my_routes, my_gates, hidden, gain_out.reshape(1, 1536), keep(near), *far)
    return lax.all_to_all(finished, "tp", 0, 0, tiled=True).reshape(512, 192)


def solution(mesh):
    fine = Mesh(mesh.devices.reshape(8, 2, 4, 4, 2), ("tp",) + EP)
    return jax.shard_map(
        per_device,
        mesh=fine,
        in_specs=(
            P(EP, "tp"),
            P(EP, "tp"),
            P("tp", EP),
            P(),
            P(),
            P(EP, None),
            P(EP, None),
            P(EP, None, None),
            P(EP, None, None),
            P(EP, None, None),
        ),
        out_specs=P(EP, "tp"),
        check_vma=False,
    )
```

```python
import jax
import jax.numpy as jnp
from jax import lax
from jax.experimental import pallas as pl
from jax.experimental.pallas import tpu as pltpu
from jax.sharding import Mesh, PartitionSpec as P

EXPERTS = 40
CAP = 16
EPS = 1e-05
BF = jnp.bfloat16
F32 = jnp.float32
EP = ("h", "y", "x", "c")
VMEM = 56 * 1024 * 1024


def params():
    return pltpu.CompilerParams(vmem_limit_bytes=VMEM)


def dot(a, b, ca, cb):
    return lax.dot_general(a, b, (((ca,), (cb,)), ((), ())), preferred_element_type=F32)


def project_kernel(place_ref, attn_ref, resid_ref, w_ref, out_ref):
    tp = place_ref[4]
    weights = w_ref[...].reshape(1536, 192)
    at = lax.broadcasted_iota(jnp.int32, (1536, 192), 0)
    of = lax.broadcasted_iota(jnp.int32, (1536, 192), 1)
    choose = jnp.where(at == of + tp * 192, 1.0, 0.0).astype(BF)
    part = dot(attn_ref[...].T, weights, 1, 1) + dot(resid_ref[...].T, choose, 1, 1)
    out_ref[...] = part.astype(BF).reshape(8, 64, 1536)


def piece_kernel(place_ref, wg_ref, wu_ref, wd_ref, out_ref):
    out_ref[0:48, :] = wg_ref[0]
    out_ref[48:96, :] = wu_ref[0]
    for i in range(3):
        out_ref[96 + i * 16 : 112 + i * 16, :] = wd_ref[0, :, i * 512 : (i + 1) * 512]


def one_hot_rows(routed, expert, rank_of):
    hits = jnp.zeros((routed.shape[0], expert.shape[1]), F32)
    for k in range(8):
        hits = hits + jnp.where(routed[:, k : k + 1] == expert, 1.0, 0.0)
    ranks = dot(rank_of, hits.astype(BF), 1, 0)
    return hits, ranks


def before_matrix(rows):
    a = lax.broadcasted_iota(jnp.int32, (rows, rows), 0)
    b = lax.broadcasted_iota(jnp.int32, (rows, rows), 1)
    keep = (b < a) & (a // 64 == b // 64)
    return jnp.where(keep, 1.0, 0.0).astype(BF)


def lane_experts(place_ref, lane):
    half, me = place_ref[3], place_ref[5]
    slot = lane // CAP
    near = (32 * half + slot) % EXPERTS
    far = 32 - 8 * half + (me + slot) % 8
    return jnp.where(slot < 32, near, far).astype(F32)


def mix_kernel(place_ref, part_ref, routes_ref, gain_ref, send_ref, hid_ref, *far_refs):
    hidden = part_ref[0].astype(F32)
    for z in range(1, 8):
        hidden = hidden + part_ref[z].astype(F32)
    hid_ref[...] = hidden
    mean = jnp.sum(hidden * hidden, axis=1, keepdims=True) / 1536
    normed = (hidden * lax.rsqrt(mean + EPS) * gain_ref[...]).astype(BF)
    lane = lax.broadcasted_iota(jnp.int32, (1, 640), 1)
    hits, ranks = one_hot_rows(routes_ref[...].astype(F32), lane_experts(place_ref, lane), before_matrix(64))
    pick = jnp.where(ranks == (lane % CAP).astype(F32), hits, 0.0).astype(BF)
    far = dot(pick[:, 512:640], normed, 0, 0).astype(BF)
    for k in range(8):
        far_refs[k][...] = far[k * CAP : (k + 1) * CAP]
    send_ref[...] = dot(pick[:, 0:512], normed, 0, 0).astype(BF).reshape(32, CAP, 1536)


def expert(x, w_gate, w_up, w_down):
    gate = dot(x, w_gate, 1, 0)
    up = dot(x, w_up, 1, 0)
    act = (gate / (1.0 + jnp.exp(-gate)) * up).astype(BF)
    return dot(act, w_down, 1, 0).astype(BF)


def near_kernel(x_ref, wg_ref, wu_ref, wd_ref, out_ref):
    half = pl.ds(pl.program_id(0) * 16, 16)
    y = expert(x_ref[half].reshape(256, 1536), wg_ref[0], wu_ref[0], wd_ref[0])
    out_ref[...] = y.reshape(16, CAP, 1536)


def far_kernel(*refs):
    x_refs, w_ref, out_refs, (wg_scr, wu_scr, wd_scr) = refs[0:8], refs[8], refs[9:17], refs[17:]
    for z in range(8):
        for q in range(4):
            block, at = z * 4 + q, q * 144
            wg_scr[block * 48 : (block + 1) * 48, :] = w_ref[z, at : at + 48, :]
            wu_scr[block * 48 : (block + 1) * 48, :] = w_ref[z, at + 48 : at + 96, :]
            for i in range(3):
                down = w_ref[z, at + 96 + i * 16 : at + 112 + i * 16, :]
                wd_scr[block * 16 : (block + 1) * 16, i * 512 : (i + 1) * 512] = down
    x = jnp.concatenate([ref[...] for ref in x_refs], axis=0)
    y = expert(x, wg_scr[...], wu_scr[...], wd_scr[...])
    for k in range(8):
        out_refs[k][...] = y[k * CAP : (k + 1) * CAP]


def close_kernel(place_ref, routes_ref, gates_ref, hid_ref, gain_ref, near_ref, *refs):
    far_refs, out_ref = refs[0:8], refs[8]
    lane = lax.broadcasted_iota(jnp.int32, (1, 640), 1)
    expert_of = lane_experts(place_ref, lane)
    routed = routes_ref[...].astype(F32)
    hits, ranks = one_hot_rows(routed, expert_of, before_matrix(64))
    gate = jnp.zeros((64, 640), F32)
    for k in range(8):
        gate = gate + jnp.where(routed[:, k : k + 1] == expert_of, gates_ref[:, k : k + 1], 0.0)
    gate = jnp.where((ranks == (lane % CAP).astype(F32)) & (hits > 0.5), gate, 0.0)
    high = gate.astype(BF)
    low = (gate - high.astype(F32)).astype(BF)
    both = jnp.concatenate([high, low], axis=0)
    far = jnp.concatenate([ref[...] for ref in far_refs], axis=0)
    total = dot(both[:, 0:512], near_ref[...].reshape(512, 1536), 1, 0) + dot(both[:, 512:640], far, 1, 0)
    combined = hid_ref[...] + (total[0:64] + total[64:128])
    mean = jnp.sum(combined * combined, axis=1, keepdims=True) / 1536
    out = (combined * lax.rsqrt(mean + EPS) * gain_ref[...]).astype(BF)
    for z in range(8):
        out_ref[z] = out[:, z * 192 : (z + 1) * 192]


def smem():
    return pl.BlockSpec(memory_space=pltpu.SMEM)


def vmem():
    return pl.BlockSpec(memory_space=pltpu.VMEM)


def keep(value):
    return pltpu.with_memory_space_constraint(value, pltpu.VMEM)


def per_device(attn, resid, w_out, gain_mix, gain_out, routes, gates, w_gate, w_up, w_down):
    tp, h, y = lax.axis_index("tp"), lax.axis_index("h"), lax.axis_index("y")
    core, me = lax.axis_index("c"), lax.axis_index(("x", "c"))
    place = jnp.stack([core, h * 4 + y, y, h, tp, me])
    shape = jax.ShapeDtypeStruct
    my_routes = lax.dynamic_slice_in_dim(routes, tp * 64, 64, 0)
    my_gates = lax.dynamic_slice_in_dim(gates, tp * 64, 64, 0)

    piece = pl.pallas_call(
        piece_kernel,
        grid_spec=pltpu.PrefetchScalarGridSpec(
            num_scalar_prefetch=1,
            grid=(4,),
            in_specs=[
                pl.BlockSpec((1, 48, 512), lambda i, p: (0, p[4] * 4 + i, 0)),
                pl.BlockSpec((1, 48, 512), lambda i, p: (0, p[4] * 4 + i, 0)),
                pl.BlockSpec((1, 16, 1536), lambda i, p: (0, p[4] * 4 + i, 0)),
            ],
            out_specs=pl.BlockSpec((144, 512), lambda i, p: (i, 0)),
        ),
        out_shape=shape((576, 512), BF),
        compiler_params=params(),
        name="piece",
    )(place, w_gate, w_up, w_down)
    crossed = lax.ppermute(piece, ("h", "y"), [(4, 3), (3, 4)])
    columns = lax.all_to_all(jnp.broadcast_to(w_out.T[None], (64, 24, 192)), EP, 0, 0, tiled=True)
    pieces = lax.all_gather(crossed, "y", axis=0, tiled=False)

    parts = pl.pallas_call(
        project_kernel,
        out_shape=shape((8, 64, 1536), BF),
        in_specs=[smem()] + [vmem()] * 3,
        out_specs=vmem(),
        compiler_params=params(),
        name="project",
    )(place, attn.T, resid.T, keep(columns))
    parts = lax.all_to_all(parts, "tp", 0, 0, tiled=True)
    rows = shape((CAP, 1536), BF)
    send, hidden, *far = pl.pallas_call(
        mix_kernel,
        out_shape=(shape((32, CAP, 1536), BF), shape((64, 1536), F32)) + (rows,) * 8,
        in_specs=[smem()] + [vmem()] * 3,
        out_specs=(vmem(),) * 10,
        compiler_params=params(),
        name="mix",
    )(place, keep(parts), my_routes, gain_mix.reshape(1, 1536))

    pieces, _ = lax.optimization_barrier((pieces, send))
    far_piece = lax.dynamic_index_in_dim(pieces, 3 - 3 * h, 0, keepdims=False)
    far_weights = lax.all_gather(far_piece, "tp", axis=0, tiled=False)

    shift = lambda v, k: lax.ppermute(v, ("x", "c"), [(i, (i + k) % 8) for i in range(8)])
    far = far[0:1] + [shift(far[k], k) for k in range(1, 8)]
    received = lax.all_to_all(send, ("y", "x", "c"), 0, 0, tiled=True)
    received, far = lax.optimization_barrier((received, far))

    near = pl.pallas_call(
        near_kernel,
        grid=(2,),
        out_shape=shape((32, CAP, 1536), BF),
        in_specs=[vmem()] * 4,
        out_specs=pl.BlockSpec((16, CAP, 1536), lambda i: (i, 0, 0)),
        compiler_params=pltpu.CompilerParams(vmem_limit_bytes=40 * 1024 * 1024),
        name="near",
    )(keep(received), keep(w_gate), w_up, w_down)
    far = pl.pallas_call(
        far_kernel,
        out_shape=(rows,) * 8,
        in_specs=[vmem()] * 9,
        out_specs=(vmem(),) * 8,
        scratch_shapes=[pltpu.VMEM((1536, 512), BF), pltpu.VMEM((1536, 512), BF), pltpu.VMEM((512, 1536), BF)],
        compiler_params=params(),
        name="far",
    )(*far, far_weights)
    near = lax.all_to_all(near, ("y", "x", "c"), 0, 0, tiled=True)
    far = [far[0]] + [shift(far[k], 8 - k) for k in range(1, 8)]

    finished = pl.pallas_call(
        close_kernel,
        out_shape=shape((8, 64, 192), BF),
        in_specs=[smem()] + [vmem()] * 13,
        out_specs=vmem(),
        compiler_params=params(),
        name="close",
    )(place, my_routes, my_gates, hidden, gain_out.reshape(1, 1536), keep(near), *far)
    return lax.all_to_all(finished, "tp", 0, 0, tiled=True).reshape(512, 192)


def solution(mesh):
    fine = Mesh(mesh.devices.reshape(8, 2, 4, 4, 2), ("tp",) + EP)
    return jax.shard_map(
        per_device,
        mesh=fine,
        in_specs=(
            P(EP, "tp"),
            P(EP, "tp"),
            P("tp", EP),
            P(),
            P(),
            P(EP, None),
            P(EP, None),
            P(EP, None, None),
            P(EP, None, None),
            P(EP, None, None),
        ),
        out_specs=P(EP, "tp"),
        check_vma=False,
    )
```

```python
import jax
import jax.numpy as jnp
from jax import lax
from jax.experimental import pallas as pl
from jax.experimental.pallas import tpu as pltpu
from jax.sharding import Mesh, PartitionSpec as P

EXPERTS = 40
CAP = 16
EPS = 1e-05
BF = jnp.bfloat16
F32 = jnp.float32
EP = ("h", "y", "x", "c")
VMEM = 56 * 1024 * 1024


def params():
    return pltpu.CompilerParams(vmem_limit_bytes=VMEM)


def dot(a, b, ca, cb):
    return lax.dot_general(a, b, (((ca,), (cb,)), ((), ())), preferred_element_type=F32)


def project_kernel(place_ref, attn_ref, resid_ref, w_ref, out_ref):
    tp = place_ref[4]
    weights = w_ref[...].reshape(1536, 192)
    at = lax.broadcasted_iota(jnp.int32, (1536, 192), 0)
    of = lax.broadcasted_iota(jnp.int32, (1536, 192), 1)
    choose = jnp.where(at == of + tp * 192, 1.0, 0.0).astype(BF)
    part = dot(attn_ref[...].T, weights, 1, 1) + dot(resid_ref[...].T, choose, 1, 1)
    out_ref[...] = part.astype(BF).reshape(8, 64, 1536)


def piece_kernel(place_ref, wg_ref, wu_ref, wd_ref, out_ref):
    out_ref[0:192, :] = wg_ref[0]
    out_ref[192:384, :] = wu_ref[0]
    for i in range(3):
        out_ref[384 + i * 64 : 448 + i * 64, :] = wd_ref[0, :, i * 512 : (i + 1) * 512]


def one_hot_rows(routed, expert, rank_of):
    hits = jnp.zeros((routed.shape[0], expert.shape[1]), F32)
    for k in range(8):
        hits = hits + jnp.where(routed[:, k : k + 1] == expert, 1.0, 0.0)
    ranks = dot(rank_of, hits.astype(BF), 1, 0)
    return hits, ranks


def before_matrix(rows):
    a = lax.broadcasted_iota(jnp.int32, (rows, rows), 0)
    b = lax.broadcasted_iota(jnp.int32, (rows, rows), 1)
    keep = (b < a) & (a // 64 == b // 64)
    return jnp.where(keep, 1.0, 0.0).astype(BF)


def lane_experts(place_ref, lane):
    half, me = place_ref[3], place_ref[5]
    slot = lane // CAP
    near = (32 * half + slot) % EXPERTS
    far = 32 - 8 * half + (me + slot) % 8
    return jnp.where(slot < 32, near, far).astype(F32)


def mix_kernel(place_ref, part_ref, routes_ref, gain_ref, send_ref, hid_ref, *far_refs):
    hidden = part_ref[0].astype(F32)
    for z in range(1, 8):
        hidden = hidden + part_ref[z].astype(F32)
    hid_ref[...] = hidden
    mean = jnp.sum(hidden * hidden, axis=1, keepdims=True) / 1536
    normed = (hidden * lax.rsqrt(mean + EPS) * gain_ref[...]).astype(BF)
    lane = lax.broadcasted_iota(jnp.int32, (1, 640), 1)
    hits, ranks = one_hot_rows(routes_ref[...].astype(F32), lane_experts(place_ref, lane), before_matrix(64))
    pick = jnp.where(ranks == (lane % CAP).astype(F32), hits, 0.0).astype(BF)
    far = dot(pick[:, 512:640], normed, 0, 0).astype(BF)
    for k in range(8):
        far_refs[k][...] = far[k * CAP : (k + 1) * CAP]
    send_ref[...] = dot(pick[:, 0:512], normed, 0, 0).astype(BF).reshape(32, CAP, 1536)


def expert(x, w_gate, w_up, w_down):
    gate = dot(x, w_gate, 1, 0)
    up = dot(x, w_up, 1, 0)
    act = (gate / (1.0 + jnp.exp(-gate)) * up).astype(BF)
    return dot(act, w_down, 1, 0).astype(BF)


def near_kernel(x_ref, wg_ref, wu_ref, wd_ref, out_ref):
    half = pl.ds(pl.program_id(0) * 16, 16)
    y = expert(x_ref[half].reshape(256, 1536), wg_ref[0], wu_ref[0], wd_ref[0])
    out_ref[...] = y.reshape(16, CAP, 1536)


def far_kernel(*refs):
    x_refs, w_ref, out_refs, (wg_scr, wu_scr, wd_scr) = refs[0:8], refs[8], refs[9:17], refs[17:]
    for z in range(8):
        wg_scr[z * 192 : (z + 1) * 192, :] = w_ref[z, 0:192, :]
        wu_scr[z * 192 : (z + 1) * 192, :] = w_ref[z, 192:384, :]
        for i in range(3):
            wd_scr[z * 64 : (z + 1) * 64, i * 512 : (i + 1) * 512] = w_ref[z, 384 + i * 64 : 448 + i * 64, :]
    x = jnp.concatenate([ref[...] for ref in x_refs], axis=0)
    y = expert(x, wg_scr[...], wu_scr[...], wd_scr[...])
    for k in range(8):
        out_refs[k][...] = y[k * CAP : (k + 1) * CAP]


def close_kernel(place_ref, routes_ref, gates_ref, hid_ref, gain_ref, near_ref, *refs):
    far_refs, out_ref = refs[0:8], refs[8]
    lane = lax.broadcasted_iota(jnp.int32, (1, 640), 1)
    expert_of = lane_experts(place_ref, lane)
    routed = routes_ref[...].astype(F32)
    hits, ranks = one_hot_rows(routed, expert_of, before_matrix(64))
    gate = jnp.zeros((64, 640), F32)
    for k in range(8):
        gate = gate + jnp.where(routed[:, k : k + 1] == expert_of, gates_ref[:, k : k + 1], 0.0)
    gate = jnp.where((ranks == (lane % CAP).astype(F32)) & (hits > 0.5), gate, 0.0)
    high = gate.astype(BF)
    low = (gate - high.astype(F32)).astype(BF)
    both = jnp.concatenate([high, low], axis=0)
    far = jnp.concatenate([ref[...] for ref in far_refs], axis=0)
    total = dot(both[:, 0:512], near_ref[...].reshape(512, 1536), 1, 0) + dot(both[:, 512:640], far, 1, 0)
    combined = hid_ref[...] + (total[0:64] + total[64:128])
    mean = jnp.sum(combined * combined, axis=1, keepdims=True) / 1536
    out = (combined * lax.rsqrt(mean + EPS) * gain_ref[...]).astype(BF)
    for z in range(8):
        out_ref[z] = out[:, z * 192 : (z + 1) * 192]


def smem():
    return pl.BlockSpec(memory_space=pltpu.SMEM)


def vmem():
    return pl.BlockSpec(memory_space=pltpu.VMEM)


def keep(value):
    return pltpu.with_memory_space_constraint(value, pltpu.VMEM)


def per_device(attn, resid, w_out, gain_mix, gain_out, routes, gates, w_gate, w_up, w_down):
    tp, h, y = lax.axis_index("tp"), lax.axis_index("h"), lax.axis_index("y")
    core, me = lax.axis_index("c"), lax.axis_index(("x", "c"))
    place = jnp.stack([core, h * 4 + y, y, h, tp, me])
    shape = jax.ShapeDtypeStruct
    my_routes = lax.dynamic_slice_in_dim(routes, tp * 64, 64, 0)
    my_gates = lax.dynamic_slice_in_dim(gates, tp * 64, 64, 0)

    piece = pl.pallas_call(
        piece_kernel,
        grid_spec=pltpu.PrefetchScalarGridSpec(
            num_scalar_prefetch=1,
            grid=(1,),
            in_specs=[
                pl.BlockSpec((1, 192, 512), lambda i, p: (0, p[4], 0)),
                pl.BlockSpec((1, 192, 512), lambda i, p: (0, p[4], 0)),
                pl.BlockSpec((1, 64, 1536), lambda i, p: (0, p[4], 0)),
            ],
            out_specs=pl.BlockSpec((576, 512), lambda i, p: (0, 0)),
        ),
        out_shape=shape((576, 512), BF),
        compiler_params=params(),
        name="piece",
    )(place, w_gate, w_up, w_down)
    crossed = lax.ppermute(piece, ("h", "y"), [(4, 3), (3, 4)])
    columns = lax.all_to_all(jnp.broadcast_to(w_out.T[None], (64, 24, 192)), EP, 0, 0, tiled=True)
    pieces = lax.all_gather(crossed, "y", axis=0, tiled=False)

    parts = pl.pallas_call(
        project_kernel,
        out_shape=shape((8, 64, 1536), BF),
        in_specs=[smem()] + [vmem()] * 3,
        out_specs=vmem(),
        compiler_params=params(),
        name="project",
    )(place, attn.T, resid.T, keep(columns))
    parts = lax.all_to_all(parts, "tp", 0, 0, tiled=True)
    rows = shape((CAP, 1536), BF)
    send, hidden, *far = pl.pallas_call(
        mix_kernel,
        out_shape=(shape((32, CAP, 1536), BF), shape((64, 1536), F32)) + (rows,) * 8,
        in_specs=[smem()] + [vmem()] * 3,
        out_specs=(vmem(),) * 10,
        compiler_params=params(),
        name="mix",
    )(place, keep(parts), my_routes, gain_mix.reshape(1, 1536))

    pieces, _ = lax.optimization_barrier((pieces, send))
    far_piece = lax.dynamic_index_in_dim(pieces, 3 - 3 * h, 0, keepdims=False)
    far_weights = lax.all_gather(far_piece, "tp", axis=0, tiled=False)

    shift = lambda v, k: lax.ppermute(v, ("x", "c"), [(i, (i + k) % 8) for i in range(8)])
    far = far[0:1] + [shift(far[k], k) for k in range(1, 8)]
    received = lax.all_to_all(send, ("y", "x", "c"), 0, 0, tiled=True)
    received, far = lax.optimization_barrier((received, far))

    near = pl.pallas_call(
        near_kernel,
        grid=(2,),
        out_shape=shape((32, CAP, 1536), BF),
        in_specs=[vmem()] * 4,
        out_specs=pl.BlockSpec((16, CAP, 1536), lambda i: (i, 0, 0)),
        compiler_params=pltpu.CompilerParams(vmem_limit_bytes=40 * 1024 * 1024),
        name="near",
    )(keep(received), keep(w_gate), w_up, w_down)
    far = pl.pallas_call(
        far_kernel,
        out_shape=(rows,) * 8,
        in_specs=[vmem()] * 9,
        out_specs=(vmem(),) * 8,
        scratch_shapes=[pltpu.VMEM((1536, 512), BF), pltpu.VMEM((1536, 512), BF), pltpu.VMEM((512, 1536), BF)],
        compiler_params=params(),
        name="far",
    )(*far, far_weights)
    near = lax.all_to_all(near, ("y", "x", "c"), 0, 0, tiled=True)
    far = [far[0]] + [shift(far[k], 8 - k) for k in range(1, 8)]

    finished = pl.pallas_call(
        close_kernel,
        out_shape=shape((8, 64, 192), BF),
        in_specs=[smem()] + [vmem()] * 13,
        out_specs=vmem(),
        compiler_params=params(),
        name="close",
    )(place, my_routes, my_gates, hidden, gain_out.reshape(1, 1536), keep(near), *far)
    return lax.all_to_all(finished, "tp", 0, 0, tiled=True).reshape(512, 192)


def solution(mesh):
    fine = Mesh(mesh.devices.reshape(8, 2, 4, 4, 2), ("tp",) + EP)
    return jax.shard_map(
        per_device,
        mesh=fine,
        in_specs=(
            P(EP, "tp"),
            P(EP, "tp"),
            P("tp", EP),
            P(),
            P(),
            P(EP, None),
            P(EP, None),
            P(EP, None, None),
            P(EP, None, None),
            P(EP, None, None),
        ),
        out_specs=P(EP, "tp"),
        check_vma=False,
    )
```
